32 devices in a mesh: dp: 16 (over z, x, core), tensor: 2 (over y).
Axes of the slice: x: 2, y: 2, z: 4, core: 2. Of those that a mesh axis runs over, the one named last changes fastest.
Arguments:
- block_input: bfloat16 [8192, 1024], P(('dp', 'tensor')), may hold values from -6 to 6
- first_layer_values: bfloat16 [8192, 1024], P('dp', 'tensor'), may hold values from -6 to 6
- segments: int32 [16, 512], P('dp'), may hold values from 0 to 1, as said below
- valid: int32 [16, 512], replicated, may hold values 0 or 1
- cotangent: bfloat16 [8192, 1024], P(('dp', 'tensor')), may hold values from -6 to 6
- teacher: bfloat16 [8192, 1024], P(('dp', 'tensor')), may hold values from -6 to 6
- layer_norm_gain: float32 [2, 1024], replicated, may hold values from 0.1 to 1.9
- layer_norm_bias: float32 [2, 1024], replicated, may hold values from -2 to 2
- lerps: float32 [7, 1024], replicated, may hold values from 0.05 to 0.95
- decay_offset: float32 [1024], replicated, may hold values from -7 to -1
- head_gain_table: float32 [3, 1024], replicated, may hold values from 0.1 to 1.9
- per_unit_shift_array: float32 [4, 1024], replicated, may hold values from -3 to 3
- lowrank_first_maps: bfloat16 [1024, 288], replicated, may hold values from -0.1875 to 0.1875
- lowrank_second_maps: bfloat16 [288, 1024], replicated, may hold values from -0.75 to 0.75
- receptance_key_value_weight: bfloat16 [3, 1024, 1024], P(None, 'dp', 'tensor'), may hold values from -0.1875 to 0.1875
- time_output_weight: bfloat16 [1024, 1024], P('tensor', 'dp'), may hold values from -0.1875 to 0.1875
- channel_key_weight: bfloat16 [1024, 4096], P('dp', 'tensor'), may hold values from -0.1875 to 0.1875
- channel_value_weight: bfloat16 [4096, 1024], P('tensor', 'dp'), may hold values from -0.09375 to 0.09375
Outputs:
- block_out: bfloat16 [8192, 1024], P(('dp', 'tensor'))
- loss: float32 [], replicated
- grad_in: float32 [8192, 1024], P(('dp', 'tensor'))
- grad_v_first: float32 [8192, 1024], P('dp', 'tensor')
- grad_norm_gain: float32 [2, 1024], replicated
- grad_norm_bias: float32 [2, 1024], replicated
- grad_lerps: float32 [6, 1024], replicated
- grad_decay_lerp: float32 [1024], replicated
- grad_decay_base: float32 [1024], replicated
- grad_head_gain: float32 [3, 1024], replicated
- grad_head_bias: float32 [4, 1024], replicated
- grad_lora_down: float32 [1024, 288], replicated
- grad_lora_up: float32 [288, 1024], replicated
- grad_rkv: float32 [3, 1024, 1024], P(None, 'dp', 'tensor')
- grad_out_weight: float32 [1024, 1024], P('tensor', 'dp')
- grad_key_weight: float32 [1024, 4096], P('dp', 'tensor')
- grad_value_weight: float32 [4096, 1024], P('tensor', 'dp')
The draws below stay inside these ranges and needn't reach their ends.
Inputs may be any that keep to these rules, and one draw needn't show every extreme that they name: `segments`: segment numbers start at 0 and rise by one from document to document along a sequence; every sequence holds max(2, 2) documents, each of at least min(60, 512 // (2 * max(2, 2))) and at most min(800, 384) tokens, and one of exactly that most.
All inputs are finite; a program needn't handle non-finite values.
Results may differ from the reference program's by a relative error of at most 0.017.
Values may be sent and summed in bfloat16 or wider, within the bound.
No kernel may reach another device: no remote copies, remote signals or barrier semaphores. Data moves between devices by JAX's collectives and lax.ppermute only.
A program may use at most 448 MiB of HBM per device.

```python
import jax
import jax.numpy as jnp
from jax import lax

MODEL_DIM = 1024
HEAD_SIZE = 64
FF = 4096
DECAY_MAP_RANK = 64
RATE_MAP_RANK = 64
VALUE_MIX_RANK = 32
GATE_MAP_RANK = 128
SPAN = 16
SEQ_LEN = 512
TOKENS = 8192
ROWS = 16
N_DP = 16


def draw_segments(key, part):
    doc_count = max(2, SEQ_LEN // 256)
    longest = min(800, SEQ_LEN * 3 // 4)
    shortest = min(60, SEQ_LEN // (2 * doc_count))
    spare = SEQ_LEN - longest - shortest * (doc_count - 1)
    key_one, key_two = jax.random.split(jax.random.fold_in(key, 11))
    weight_set = jax.random.randint(key_one, (ROWS, doc_count - 1), 50, 101).astype(jnp.int32)
    totals = jnp.sum(weight_set, -1, keepdims=True)
    shares = spare * weight_set // totals
    leftover = spare - jnp.sum(shares, -1)
    shares = shares.at[:, -1].add(leftover)
    others = (shortest + shares).astype(jnp.int32)
    spot = jax.random.randint(key_two, (ROWS, 1), 0, doc_count).astype(jnp.int32)
    places = jnp.arange(doc_count, dtype=jnp.int32)[None, :]
    zero_col = jnp.zeros((ROWS, 1), jnp.int32)
    before = jnp.concatenate([others, zero_col], 1)
    after = jnp.concatenate([zero_col, others], 1)
    lengths = jnp.where(places == spot, longest, jnp.where(places < spot, before, after)).astype(jnp.int32)
    ends = jnp.cumsum(lengths, -1).astype(jnp.int32)
    positions = jnp.arange(SEQ_LEN, dtype=jnp.int32)
    return jnp.sum((positions[None, :, None] >= ends[:, None, :]).astype(jnp.int32), -1).astype(jnp.int32)


def touch_ends(drawn, stream_key, low, high):
    longest = drawn.shape.index(max(drawn.shape))
    spots = []
    for shift in (0, 1):
        where = [jax.random.randint(jax.random.fold_in(stream_key, axis), (), 0, length) for axis, length in enumerate(drawn.shape)]
        where[longest] = (where[longest] + shift) % drawn.shape[longest]
        spots.append(tuple(where))
    return drawn.at[spots[0]].set(low).at[spots[1]].set(high)


def block_levels(stream_key, dims, shards, smallest, high):
    level, own = 1.0, jax.random.fold_in(stream_key, 6)
    for axis_at, shards_of in shards:
        heights = jnp.exp(jax.random.uniform(jax.random.fold_in(own, axis_at), (shards_of,), jnp.float32, smallest / len(shards), high / len(shards)))
        level = level * jnp.repeat(heights, dims[axis_at] // shards_of).reshape([-1 if axis == axis_at else 1 for axis in range(len(dims))])
    return level


def normal_values(rng, dims, width, reach, pieces=(), held_as=jnp.bfloat16):
    level = block_levels(rng, dims, pieces, -0.22, 0.18) if pieces else 1.0
    entries = jax.random.normal(rng, dims, jnp.float32) * width * level
    return jnp.minimum(jnp.maximum(entries, -reach), reach).astype(held_as)


def setup_inputs(seed: int = 0) -> dict:
    seeds = jax.random.split(jax.random.key(seed), 19)
    return {
        "block_input": normal_values(seeds[0], (TOKENS, MODEL_DIM), 1.0, 6.0, ((0, 32),)),
        "first_layer_values": normal_values(seeds[1], (TOKENS, MODEL_DIM), 1.0, 6.0, ((0, 16), (1, 2))),
        "segments": draw_segments(jax.random.fold_in(seeds[18], 71), 0),
        "valid": touch_ends((jax.random.randint(seeds[3], (ROWS, SEQ_LEN), 0, 8) < 7).astype(jnp.int32), jax.random.fold_in(seeds[3], 1), 0, 1),
        "cotangent": normal_values(seeds[4], (TOKENS, MODEL_DIM), 1.0, 6.0, ((0, 32),)),
        "teacher": normal_values(seeds[5], (TOKENS, MODEL_DIM), 1.0, 6.0, ((0, 32),)),
        "layer_norm_gain": jnp.clip(1.0 + 0.18 * jax.random.normal(seeds[6], (2, MODEL_DIM), jnp.float32), 0.1, 1.9),
        "layer_norm_bias": normal_values(seeds[7], (2, MODEL_DIM), 0.3, 2.0, (), jnp.float32),
        "lerps": jnp.clip(jax.random.uniform(seeds[8], (7, MODEL_DIM), jnp.float32, 0.05, 0.95), 0.05, 0.95),
        "decay_offset": jnp.clip(jax.random.uniform(seeds[9], (MODEL_DIM,), jnp.float32, -7.0, -1.0), -7.0, -1.0),
        "head_gain_table": jnp.clip(1.0 + 0.18 * jax.random.normal(seeds[10], (3, MODEL_DIM), jnp.float32), 0.1, 1.9),
        "per_unit_shift_array": normal_values(seeds[11], (4, MODEL_DIM), 0.5, 3.0, (), jnp.float32),
        "lowrank_first_maps": normal_values(seeds[12], (MODEL_DIM, DECAY_MAP_RANK + RATE_MAP_RANK + VALUE_MIX_RANK + GATE_MAP_RANK), MODEL_DIM ** -0.5, 0.1875),
        "lowrank_second_maps": normal_values(seeds[13], (DECAY_MAP_RANK + RATE_MAP_RANK + VALUE_MIX_RANK + GATE_MAP_RANK, MODEL_DIM), DECAY_MAP_RANK ** -0.5, 0.75),
        "receptance_key_value_weight": normal_values(seeds[14], (3, MODEL_DIM, MODEL_DIM), MODEL_DIM ** -0.5, 0.1875, ((1, 16), (2, 2))),
        "time_output_weight": normal_values(seeds[15], (MODEL_DIM, MODEL_DIM), MODEL_DIM ** -0.5, 0.1875, ((0, 2), (1, 16))),
        "channel_key_weight": normal_values(seeds[16], (MODEL_DIM, FF), MODEL_DIM ** -0.5, 0.1875, ((0, 16), (1, 2))),
        "channel_value_weight": normal_values(seeds[17], (FF, MODEL_DIM), FF ** -0.5, 0.09375, ((0, 2), (1, 16))),
    }


@jax.custom_vjp
def lowrank_hidden(v):
    return lax.optimization_barrier(v.astype(jnp.bfloat16)).astype(jnp.float32)

@jax.custom_vjp
def lowrank_reverse(v):
    return v

def low_keep(v):
    return (lowrank_hidden(v), None)

def low_pass(kept, grad):
    return (grad,)

def back_keep(v):
    return (v, None)

def back_low(kept, grad):
    return (lowrank_hidden(grad),)
lowrank_hidden.defvjp(low_keep, low_pass)
lowrank_reverse.defvjp(back_keep, back_low)

def multiplied(left, right):
    return jnp.dot(left, right, precision=lax.Precision.HIGHEST)

def layer_norm(row_data, gain_row, bias_row):
    row_mean = lax.optimization_barrier(jnp.mean(row_data, -1, keepdims=True))
    centred = row_data - row_mean
    variance = lax.optimization_barrier(jnp.mean(centred * centred, -1, keepdims=True))
    return centred * lax.rsqrt(variance + 1e-05) * gain_row + bias_row

def shifted(row_data, retain_mask):
    return jnp.concatenate([jnp.zeros_like(row_data[:1]), row_data[:-1]], 0) * retain_mask[:, None]

def token_step(wkv_state, inputs):
    acceptance_vector_lines, key_row, value_row, decay_logarithm, removal, rate_row, keep_gate = inputs
    wkv_state = wkv_state * keep_gate
    removed = jnp.einsum('hvk,hk->hv', wkv_state, removal, precision=lax.Precision.HIGHEST)
    wkv_state = wkv_state * jnp.exp(decay_logarithm)[:, None, :] - removed[:, :, None] * (removal * rate_row)[:, None, :] + value_row[:, :, None] * key_row[:, None, :]
    return (wkv_state, jnp.einsum('hvk,hk->hv', wkv_state, acceptance_vector_lines, precision=lax.Precision.HIGHEST))

def run_block(wkv_state, inputs):
    return lax.scan(token_step, wkv_state, inputs)

def recurrence(acceptance_vector_lines, lookup_vector_stripe, payload_vector_lines, decay_logarithm, removal, context_rates, retain_mask):
    entire_sample_lines = acceptance_vector_lines.shape[0]
    head_count = acceptance_vector_lines.shape[1]
    blocks = entire_sample_lines // SPAN

    def to_blocks(tensor):
        return tensor.reshape((blocks, SPAN) + tensor.shape[1:])
    keep_gates = retain_mask.reshape(blocks, SPAN, 1, 1)
    wkv_state = jnp.zeros((head_count, HEAD_SIZE, HEAD_SIZE), jnp.float32)
    _, outputs = lax.scan(jax.checkpoint(run_block), wkv_state, (to_blocks(acceptance_vector_lines), to_blocks(lookup_vector_stripe), to_blocks(payload_vector_lines), to_blocks(decay_logarithm), to_blocks(removal), to_blocks(context_rates), keep_gates))
    return outputs.reshape(entire_sample_lines, head_count, HEAD_SIZE)

def time_mixer_core(acceptance_vector_lines, key_projected, value_projected, decay_lowrank, rate_lowrank, value_lowrank, output_switch_thin_factors, leading_value, decay_offset, head_gain_table, per_unit_shift_array, retain_mask):
    context_rates = jax.nn.sigmoid(per_unit_shift_array[0] + rate_lowrank)
    blending = jax.nn.sigmoid(per_unit_shift_array[1] + value_lowrank)
    payload_vector_lines = value_projected + (leading_value - value_projected) * blending
    decay_logarithm = -jnp.exp(-jax.nn.softplus(-(decay_offset + decay_lowrank)) - 0.5)
    removal = key_projected * head_gain_table[0]
    lookup_vector_stripe = key_projected * (1.0 + (context_rates - 1.0) * head_gain_table[1])
    entire_sample_lines = acceptance_vector_lines.shape[0]
    embedding_feature_span = acceptance_vector_lines.shape[1]
    head_count = embedding_feature_span // HEAD_SIZE

    def split_into_attention_units(tensor):
        return tensor.reshape(entire_sample_lines, head_count, HEAD_SIZE)
    removal = split_into_attention_units(removal)
    removal = removal * lax.rsqrt(lax.optimization_barrier(jnp.sum(removal * removal, -1, keepdims=True)) + 1e-06)
    mixed_out = recurrence(split_into_attention_units(acceptance_vector_lines), split_into_attention_units(lookup_vector_stripe), split_into_attention_units(payload_vector_lines), split_into_attention_units(decay_logarithm), removal, split_into_attention_units(context_rates), retain_mask)
    head_mean = lax.optimization_barrier(jnp.mean(mixed_out, -1, keepdims=True))
    centred = mixed_out - head_mean
    variance = lax.optimization_barrier(jnp.mean(centred * centred, -1, keepdims=True))
    standardized_result = (centred * lax.rsqrt(variance + HEAD_SIZE * 0.01)).reshape(entire_sample_lines, embedding_feature_span) * head_gain_table[2] + per_unit_shift_array[3]
    extra_reward_addend = lax.optimization_barrier(jnp.sum(split_into_attention_units(acceptance_vector_lines * lookup_vector_stripe * per_unit_shift_array[2]), -1, keepdims=True)) * split_into_attention_units(payload_vector_lines)
    return (standardized_result + extra_reward_addend.reshape(entire_sample_lines, embedding_feature_span)) * output_switch_thin_factors

def group_norm_forward(block_row_slice, leading_values, cotangent_rows, destination_rows, valid_portion, retain_portion, valid_token_count, layer_norm_gain, layer_norm_bias, lerps, decay_offset, head_gain_table, per_unit_shift_array, lowrank_first_maps, lowrank_second_maps, receptance_key_value_weight, time_output_weight, channel_key_weight, channel_value_weight):
    divide_pair = DECAY_MAP_RANK + RATE_MAP_RANK
    divide_three = divide_pair + VALUE_MIX_RANK
    normed_one = lowrank_hidden(layer_norm(block_row_slice, layer_norm_gain[0], layer_norm_bias[0]))
    delta_one = shifted(normed_one, retain_portion) - normed_one
    blended = [lowrank_hidden(normed_one + delta_one * lerps[lane_index]) for lane_index in range(6)]
    acceptance_vector_lines = lowrank_reverse(multiplied(blended[0], receptance_key_value_weight[0]))
    key_projected = lowrank_reverse(multiplied(blended[2], receptance_key_value_weight[1]))
    value_projected = lowrank_reverse(multiplied(blended[3], receptance_key_value_weight[2]))
    decay_inner = lowrank_hidden(jnp.tanh(lowrank_reverse(multiplied(blended[1], lowrank_first_maps[:, :DECAY_MAP_RANK]))))
    rate_inner = lowrank_hidden(lowrank_reverse(multiplied(blended[4], lowrank_first_maps[:, DECAY_MAP_RANK:divide_pair])))
    value_inner = lowrank_hidden(lowrank_reverse(multiplied(blended[3], lowrank_first_maps[:, divide_pair:divide_three])))
    gate_inner = lowrank_hidden(jax.nn.sigmoid(lowrank_reverse(multiplied(blended[5], lowrank_first_maps[:, divide_three:]))))
    decay_lowrank = lowrank_reverse(multiplied(decay_inner, lowrank_second_maps[:DECAY_MAP_RANK]))
    rate_lowrank = lowrank_reverse(multiplied(rate_inner, lowrank_second_maps[DECAY_MAP_RANK:divide_pair]))
    value_lowrank = lowrank_reverse(multiplied(value_inner, lowrank_second_maps[divide_pair:divide_three]))
    output_switch_thin_factors = lowrank_reverse(multiplied(gate_inner, lowrank_second_maps[divide_three:]))
    time_mixer_output = lowrank_hidden(time_mixer_core(acceptance_vector_lines, key_projected, value_projected, decay_lowrank, rate_lowrank, value_lowrank, output_switch_thin_factors, leading_values, decay_offset, head_gain_table, per_unit_shift_array, retain_portion))
    after_mixer = block_row_slice + lowrank_reverse(multiplied(time_mixer_output, time_output_weight))
    normed_two = lowrank_hidden(layer_norm(after_mixer, layer_norm_gain[1], layer_norm_bias[1]))
    channel_in = lowrank_hidden(normed_two + (shifted(normed_two, retain_portion) - normed_two) * lerps[6])
    channel_pre = lowrank_reverse(multiplied(channel_in, channel_key_weight))
    hidden_rows = lowrank_hidden(jnp.square(jax.nn.relu(channel_pre)))
    block_sum = after_mixer + lowrank_reverse(multiplied(hidden_rows, channel_value_weight))
    mismatch = block_sum - destination_rows
    loss_part = jnp.sum(valid_portion[:, None] * mismatch * mismatch) / (valid_token_count * MODEL_DIM)
    objective = jnp.sum(valid_portion[:, None] * block_sum * cotangent_rows) + loss_part
    return (objective, (block_sum, loss_part))

def reference(block_input, first_layer_values, segments, valid, cotangent, teacher, layer_norm_gain, layer_norm_bias, lerps, decay_offset, head_gain_table, per_unit_shift_array, lowrank_first_maps, lowrank_second_maps, receptance_key_value_weight, time_output_weight, channel_key_weight, channel_value_weight):
    weight_set = tuple((table_entry.astype(jnp.float32) for table_entry in (layer_norm_gain, layer_norm_bias, lerps, decay_offset, head_gain_table, per_unit_shift_array, lowrank_first_maps, lowrank_second_maps, receptance_key_value_weight, time_output_weight, channel_key_weight, channel_value_weight)))
    valid_rows = valid.astype(jnp.float32).reshape(-1)
    valid_token_count = jnp.sum(valid_rows)
    same_doc = (segments[:, 1:] == segments[:, :-1]).astype(jnp.float32)
    retain_mask = jnp.concatenate([jnp.zeros((segments.shape[0], 1), jnp.float32), same_doc], 1).reshape(-1)
    groups = N_DP

    def per_group(tensor):
        return tensor.reshape((groups, tensor.shape[0] // groups) + tensor.shape[1:])

    def visit(running, group_item):
        inputs_x, first_rows, cotangent_rows, destination_rows, valid_portion, retain_portion = group_item

        def objective(block_row_slice, leading_values, *params):
            return group_norm_forward(block_row_slice, leading_values, cotangent_rows, destination_rows, valid_portion, retain_portion, valid_token_count, *params)
        _, pullback, (out_rows, loss_part) = jax.vjp(objective, inputs_x, first_rows, *weight_set, has_aux=True)
        pulled = pullback(jnp.ones((), jnp.float32))
        running = tuple((summed + extra for summed, extra in zip(running, pulled[2:])))
        return (running, (out_rows.astype(jnp.bfloat16), loss_part, pulled[0], pulled[1]))
    initial = tuple((jnp.zeros_like(table_entry) for table_entry in weight_set))
    running, (out_rows, losses, input_grads, first_grads) = lax.scan(visit, initial, (per_group(block_input.astype(jnp.float32)), per_group(first_layer_values.astype(jnp.float32)), per_group(cotangent.astype(jnp.float32)), per_group(teacher.astype(jnp.float32)), per_group(valid_rows), per_group(retain_mask)))
    embedding_feature_span = block_input.shape[1]
    lerp_grads = running[2]
    return (out_rows.reshape(-1, embedding_feature_span), jnp.sum(losses), input_grads.reshape(-1, embedding_feature_span), first_grads.reshape(-1, embedding_feature_span), running[0], running[1], jnp.concatenate([lerp_grads[:1], lerp_grads[2:]], 0), lerp_grads[1], running[3], running[4], running[5], running[6], running[7], running[8], running[9], running[10], running[11])
```

```python
import jax
import jax.numpy as jnp
from jax import lax
from jax.experimental import pallas as pl
from jax.experimental.pallas import tpu as pltpu
from jax.sharding import PartitionSpec as P

HEAD_SIZE = 64
CHUNK = 64
PAIR = 2 * HEAD_SIZE
BF = jnp.bfloat16
F32 = jnp.float32
DECAY_SCALE = 0.6065306597126334
DECAY_MAP_RANK = 64
RATE_MAP_RANK = 64
VALUE_MIX_RANK = 32


def matrix_multiply(left, right):
    return jnp.dot(left, right, preferred_element_type=jnp.float32)


def matmul_tn(left, right):
    return lax.dot_general(
        left, right, (((0,), (0,)), ((), ())), preferred_element_type=jnp.float32
    )


def matrix_multiply_transposed(left, right):
    return lax.dot_general(
        left, right, (((1,), (1,)), ((), ())), preferred_element_type=jnp.float32
    )


def layer_norm(row_data, gain_row, bias_row):
    row_mean = jnp.mean(row_data, -1, keepdims=True)
    centred = row_data - row_mean
    variance = jnp.mean(centred * centred, -1, keepdims=True)
    return centred * lax.rsqrt(variance + 1e-05) * gain_row + bias_row


def shift_down(row_data, retain_mask):
    return jnp.concatenate([jnp.zeros_like(row_data[:1]), row_data[:-1]], 0) * retain_mask[:, None]


def shift_up(row_data, retain_mask):
    moved = row_data * retain_mask[:, None]
    return jnp.concatenate([moved[1:], jnp.zeros_like(moved[:1])], 0)


def add_rows(full_rows, extra_rows, first_row):
    current = lax.dynamic_slice_in_dim(full_rows, first_row, extra_rows.shape[0], 0)
    return lax.dynamic_update_slice_in_dim(full_rows, current + extra_rows, first_row, 0)


def place_cols(col_block, total_cols, first_col):
    zeros_full = jnp.zeros(col_block.shape[:-1] + (total_cols,), jnp.float32)
    return lax.dynamic_update_slice_in_dim(zeros_full, col_block, first_col, col_block.ndim - 1)


NN = (((1,), (0,)), ((), ()))
NT = (((1,), (1,)), ((), ()))
TN = (((0,), (0,)), ((), ()))


def split(x, terms=2):
    hi = x.astype(BF)
    if terms == 1:
        return (hi,)
    return (hi, (x - hi.astype(F32)).astype(BF))


def mm(a, b, dims):
    out = lax.dot_general(a[0], b[0], dims, preferred_element_type=F32)
    if len(b) > 1:
        out = out + lax.dot_general(a[0], b[1], dims, preferred_element_type=F32)
    if len(a) > 1:
        out = out + lax.dot_general(a[1], b[0], dims, preferred_element_type=F32)
    return out


def rows_of(*parts):
    return tuple(jnp.concatenate(terms, 0) for terms in zip(*parts))


def cols_of(*parts):
    return tuple(jnp.concatenate(terms, 1) for terms in zip(*parts))


def spread(parts, left, right):
    return tuple(jnp.concatenate([x * left, x * right], 0) for x in parts)


def chunk_masks(gcol, aux):
    size = 2 * CHUNK
    row = lax.broadcasted_iota(jnp.int32, (size, size), 0)
    lane = lax.broadcasted_iota(jnp.int32, (size, size), 1)
    t_row, t_lane = row & (CHUNK - 1), lane & (CHUNK - 1)
    same_head = (row >= CHUNK) == (lane >= CHUNK)
    g_row = jnp.concatenate([gcol, gcol], 0)
    linked = (g_row == aux[0:1, :]) & same_head
    strict = linked & (t_row > t_lane)
    upto = linked & (t_row >= t_lane)
    from_start = (gcol == aux[2:3, :]).astype(F32)
    to_end = (gcol == aux[1:2, :]).astype(F32)
    end_clear = (aux[1:2, :] == aux[2:3, :]).astype(F32)
    return row, lane, t_row, t_lane, strict, upto, from_start, to_end, end_clear


def head_sum(x, ones):
    return mm(split(x), (ones,), NN)


def lane_masks():
    lane = lax.broadcasted_iota(jnp.int32, (1, PAIR), 1)
    left = (lane < HEAD_SIZE).astype(F32)
    return left.astype(BF), (1.0 - left).astype(BF), left


def head_ones():
    row = lax.broadcasted_iota(jnp.int32, (PAIR, PAIR), 0)
    lane = lax.broadcasted_iota(jnp.int32, (PAIR, PAIR), 1)
    return ((row >= HEAD_SIZE) == (lane >= HEAD_SIZE)).astype(F32).astype(BF)


def lower_ones():
    row = lax.broadcasted_iota(jnp.int32, (CHUNK, CHUNK), 0)
    lane = lax.broadcasted_iota(jnp.int32, (CHUNK, CHUNK), 1)
    return (row >= lane).astype(F32).astype(BF)


def split3(x):
    hi = x.astype(BF)
    rest = x - hi.astype(F32)
    mid = rest.astype(BF)
    return (hi, mid, (rest - mid.astype(F32)).astype(BF))


def ones_times(ones, x, dims):
    total = None
    for term in split3(x):
        part = lax.dot_general(ones, term, dims, preferred_element_type=F32)
        total = part if total is None else total + part
    return total


def sigmoid(x):
    return jax.nn.sigmoid(x)


def pair_values(refs, par, cols, ones):
    r_ref, kp_ref, vp_ref, ew_ref, ea_ref, ev_ref, vf_ref = refs
    out = {}
    r, kp, vp = r_ref[:, cols], kp_ref[:, cols], vp_ref[:, cols]
    vf = vf_ref[:, cols].astype(F32)
    a = sigmoid(par[4:5] + ea_ref[:, cols])
    s = sigmoid(par[5:6] + ev_ref[:, cols])
    v = vp + (vf - vp) * s
    sg = sigmoid(par[0:1] + ew_ref[:, cols])
    ld = -DECAY_SCALE * sg
    u = kp * par[1:2]
    inv = lax.rsqrt(head_sum(u * u, ones) + 1e-06)
    kk = u * inv
    k = kp * (1.0 + (a - 1.0) * par[2:3])
    out.update(r=r, kp=kp, vp=vp, vf=vf, a=a, s=s, v=v, sg=sg, ld=ld, inv=inv, kk=kk, k=k)
    return out


def chunk_values(w, lower, from_start, to_end, end_clear):
    inc = ones_times(lower, w["ld"], NN)
    exc = inc - w["ld"]
    last = inc[CHUNK - 1 : CHUNK, :]
    w["e_inc"] = jnp.exp(inc)
    w["e_exc"] = jnp.exp(exc)
    w["e_neg"] = jnp.exp(-inc)
    w["carry"] = jnp.exp(last - inc) * to_end
    w["finish"] = jnp.exp(last) * end_clear
    w["b"] = w["kk"] * w["a"]
    w["kappa"] = w["kk"] * w["e_exc"]
    w["rho"] = w["r"] * w["e_inc"]
    w["key_hat"] = w["k"] * w["e_neg"]
    w["take_hat"] = w["b"] * w["e_neg"]
    w["k_end"] = w["k"] * w["carry"]
    w["b_end"] = w["b"] * w["carry"]
    w["kappa0"] = w["kappa"] * from_start
    w["rho0"] = w["rho"] * from_start


def forward_kernel(
    r_ref, kp_ref, vp_ref, ew_ref, ea_ref, ev_ref, gate_ref, vf_ref, par_ref, gcol_ref, aux_ref,
    z_ref, y_ref, q_ref, t_ref, akk_ref, ark_ref, arb_ref, s0_ref, state,
):
    pairs = r_ref.shape[1] // PAIR

    @pl.when(pl.program_id(0) == 0)
    def _():
        state[...] = jnp.zeros_like(state)

    masks = chunk_masks(gcol_ref[...], aux_ref[0])
    row, lane, t_row, t_lane, strict, upto, from_start, to_end, end_clear = masks
    left, right, left_f = lane_masks()
    ones = head_ones()
    lower = lower_ones()
    eye = (row == lane).astype(F32)
    in8 = (t_row >> 3) == (t_lane >> 3)
    levels = []
    for bits in (3, 4, 5):
        levels.append(((t_row >> (bits + 1)) == (t_lane >> (bits + 1))) & ((t_row >> bits) != (t_lane >> bits)))
    group = range(pairs)
    cols = [slice(p * PAIR, (p + 1) * PAIR) for p in group]
    refs = (r_ref, kp_ref, vp_ref, ew_ref, ea_ref, ev_ref, vf_ref)
    pars = [par_ref[:, cols[p]] for p in group]
    w = [pair_values(refs, pars[p], cols[p], ones) for p in group]
    for p in group:
        chunk_values(w[p], lower, from_start, to_end, end_clear)
    akk, akb, ark, arb = [], [], [], []
    for p in group:
        x = w[p]
        rows = rows_of(spread(split(x["kappa"]), left, right), spread(split(x["rho"]), left, right))
        keys = rows_of(spread(split(x["key_hat"]), left, right), spread(split(x["take_hat"]), left, right))
        scores = mm(rows, keys, NT)
        n = 2 * CHUNK
        akk.append(jnp.where(strict, scores[:n, :n], 0.0))
        akb.append(jnp.where(strict, scores[:n, n:], 0.0))
        ark.append(jnp.where(upto, scores[n:, :n], 0.0))
        arb.append(jnp.where(upto, scores[n:, n:], 0.0))
    neg = [jnp.where(in8, -akb[p], 0.0) for p in group]
    neg_s = [split(x) for x in neg]
    two = [mm(x, x, NN) for x in neg_s]
    two_s = [split(x) for x in two]
    both = [mm(rows_of(neg_s[p], two_s[p]), two_s[p], NN) for p in group]
    n = 2 * CHUNK
    low = [neg[p] + two[p] + both[p][:n] for p in group]
    four = [both[p][n:] for p in group]
    inv = [eye + low[p] + four[p] + mm(split(low[p]), split(four[p]), NN) for p in group]
    for level in levels:
        inv_s = [split(x) for x in inv]
        mid = [mm(split(jnp.where(level, akb[p], 0.0)), inv_s[p], NN) for p in group]
        inv = [inv[p] - mm(inv_s[p], split(mid[p]), NN) for p in group]
    inv_s = [split(x) for x in inv]
    v_s = [spread(split(w[p]["v"]), left, right) for p in group]
    akk_v = [mm(split(akk[p]), v_s[p], NN) for p in group]
    s0 = [state[p] for p in group]
    carried = [
        mm(
            rows_of(spread(split(w[p]["kappa0"]), left, right), spread(split(w[p]["rho0"]), left, right)),
            split(s0[p]),
            NT,
        )
        for p in group
    ]
    q = [mm(inv_s[p], split(carried[p][:n] + akk_v[p]), NN) for p in group]
    q_s = [split(x) for x in q]
    y2 = [
        carried[p][n:] + mm(cols_of(split(ark[p]), split(-arb[p])), rows_of(v_s[p], q_s[p]), NN)
        for p in group
    ]
    for p in group:
        x = w[p]
        ends = rows_of(spread(split(x["k_end"]), left, right), spread(split(-x["b_end"]), left, right))
        state[p] = s0[p] * x["finish"] + mm(rows_of(v_s[p], q_s[p]), ends, TN)
        y = y2[p][:CHUNK] + y2[p][CHUNK:]
        y_ref[:, cols[p]] = y
        q_ref[:, cols[p]] = q[p][:CHUNK] + q[p][CHUNK:]
        t_ref[0, p] = inv[p]
        akk_ref[0, p] = akk[p]
        ark_ref[0, p] = ark[p]
        arb_ref[0, p] = arb[p]
        s0_ref[0, p] = s0[p]
        par = pars[p]
        centred = y - head_sum(y, ones) * (1.0 / HEAD_SIZE)
        var = head_sum(centred * centred, ones) * (1.0 / HEAD_SIZE)
        normed = centred * lax.rsqrt(var + HEAD_SIZE * 0.01)
        bonus = head_sum(x["r"] * x["k"] * par[6:7], ones)
        z = (normed * par[3:4] + par[7:8] + bonus * x["v"]) * gate_ref[:, cols[p]]
        z_ref[:, cols[p]] = z.astype(z_ref.dtype)


def backward_kernel(
    dz_ref, r_ref, kp_ref, vp_ref, ew_ref, ea_ref, ev_ref, gate_ref, vf_ref, par_ref, gcol_ref, aux_ref,
    y_ref, q_ref, t_ref, akk_ref, ark_ref, arb_ref, s0_ref,
    dr_ref, dkp_ref, dvp_ref, dew_ref, dea_ref, dev_ref, dgate_ref, dvf_ref, dpar_ref, state,
):
    pairs = r_ref.shape[1] // PAIR
    n = 2 * CHUNK

    @pl.when(pl.program_id(0) == 0)
    def _():
        state[...] = jnp.zeros_like(state)
        dpar_ref[...] = jnp.zeros_like(dpar_ref)

    masks = chunk_masks(gcol_ref[...], aux_ref[0])
    row, lane, t_row, t_lane, strict, upto, from_start, to_end, end_clear = masks
    left, right, left_f = lane_masks()
    ones = head_ones()
    lower = lower_ones()
    last_row = (lax.broadcasted_iota(jnp.int32, (CHUNK, 1), 0) == CHUNK - 1).astype(F32)
    group = range(pairs)
    cols = [slice(p * PAIR, (p + 1) * PAIR) for p in group]
    refs = (r_ref, kp_ref, vp_ref, ew_ref, ea_ref, ev_ref, vf_ref)
    pars = [par_ref[:, cols[p]] for p in group]
    w = [pair_values(refs, pars[p], cols[p], ones) for p in group]
    scale = 1.0 / HEAD_SIZE
    for p in group:
        x, par = w[p], pars[p]
        chunk_values(x, lower, from_start, to_end, end_clear)
        y = y_ref[:, cols[p]]
        centred = y - head_sum(y, ones) * scale
        var = head_sum(centred * centred, ones) * scale
        istd = lax.rsqrt(var + HEAD_SIZE * 0.01)
        normed = centred * istd
        rk = x["r"] * x["k"]
        bonus = head_sum(rk * par[6:7], ones)
        dz = dz_ref[:, cols[p]]
        dgate_ref[:, cols[p]] = (dz * (normed * par[3:4] + par[7:8] + bonus * x["v"])).astype(BF)
        do = dz * gate_ref[:, cols[p]]
        dbonus = head_sum(do * x["v"], ones)
        x["dv"] = do * bonus
        x["dr"] = dbonus * x["k"] * par[6:7]
        x["dk"] = dbonus * x["r"] * par[6:7]
        dn = do * par[3:4]
        x["dy"] = istd * (dn - head_sum(dn, ones) * scale - normed * (head_sum(dn * normed, ones) * scale))
        x["g2"] = jnp.sum(do * normed, 0, keepdims=True)
        x["b3"] = jnp.sum(do, 0, keepdims=True)
        x["b2"] = jnp.sum(dbonus * rk, 0, keepdims=True)
    dy_s = [spread(split(w[p]["dy"]), left, right) for p in group]
    v_s = [spread(split(w[p]["v"]), left, right) for p in group]
    q_s = [spread(split(q_ref[:, cols[p]]), left, right) for p in group]
    ds = [state[p] for p in group]
    ds_s = [split(ds[p]) for p in group]
    kend_s = [spread(split(w[p]["k_end"]), left, right) for p in group]
    bend_s = [spread(split(w[p]["b_end"]), left, right) for p in group]
    from_end = [mm(rows_of(kend_s[p], bend_s[p]), ds_s[p], NT) for p in group]
    dq = [-(mm(split(arb_ref[0, p]), dy_s[p], TN) + from_end[p][n:]) for p in group]
    du = [mm(split(t_ref[0, p]), split(dq[p]), TN) for p in group]
    du_s = [split(du[p]) for p in group]
    uy_s = [rows_of(du_s[p], dy_s[p]) for p in group]
    s0 = [s0_ref[0, p] for p in group]
    kappa_s = [spread(split(w[p]["kappa"]), left, right) for p in group]
    rho_s = [spread(split(w[p]["rho"]), left, right) for p in group]
    for p in group:
        x = w[p]
        start = rows_of(spread(split(x["kappa0"]), left, right), spread(split(x["rho0"]), left, right))
        state[p] = ds[p] * x["finish"] + mm(uy_s[p], start, TN)
    dv2 = [
        from_end[p][:n] + mm(rows_of(split(akk_ref[0, p]), split(ark_ref[0, p])), uy_s[p], TN)
        for p in group
    ]
    start_grad = [mm(uy_s[p], split(s0[p]), NN) for p in group]
    end_grad = [mm(rows_of(v_s[p], q_s[p]), ds_s[p], NN) for p in group]
    vq_s = [rows_of(v_s[p], tuple(-t for t in q_s[p])) for p in group]
    raw = [mm(uy_s[p], vq_s[p], NT) for p in group]
    da_s = []
    for p in group:
        top = jnp.where(jnp.concatenate([strict, strict], 1), raw[p][:n], 0.0)
        bottom = jnp.where(jnp.concatenate([upto, upto], 1), raw[p][n:], 0.0)
        da_s.append(split(jnp.concatenate([top, bottom], 0)))
    row_grad = [
        mm(
            da_s[p],
            rows_of(spread(split(w[p]["key_hat"]), left, right), spread(split(w[p]["take_hat"]), left, right)),
            NN,
        )
        for p in group
    ]
    col_grad = [mm(da_s[p], rows_of(kappa_s[p], rho_s[p]), TN) for p in group]

    def fold(z):
        return z[:CHUNK] + z[CHUNK:n], z[n : n + CHUNK] + z[n + CHUNK :]

    for p in group:
        x, par = w[p], pars[p]
        dkappa0, drho0 = fold(start_grad[p])
        dkend, dbend = fold(end_grad[p])
        dbend = -dbend
        dkappa, drho = fold(row_grad[p])
        dkey, dtake = fold(col_grad[p])
        dkappa = dkappa + dkappa0 * from_start
        drho = drho + drho0 * from_start
        dv = x["dv"] + dv2[p][:CHUNK] + dv2[p][CHUNK:]
        dr = x["dr"] + drho * x["e_inc"]
        dk = x["dk"] + dkey * x["e_neg"] + dkend * x["carry"]
        db = dtake * x["e_neg"] + dbend * x["carry"]
        dkk = dkappa * x["e_exc"] + db * x["a"]
        da = db * x["kk"]
        dexc = dkappa * x["kappa"]
        dends = dkend * x["k_end"] + dbend * x["b_end"]
        dinc = drho * x["rho"] - dkey * x["key_hat"] - dtake * x["take_hat"] - dends
        dlast = jnp.sum(dends, 0, keepdims=True) + jnp.sum(s0[p] * ds[p], 0, keepdims=True) * x["finish"]
        dld = ones_times(lower, dinc + dexc + last_row * dlast, TN) - dexc
        dkp = dk * (1.0 + (x["a"] - 1.0) * par[2:3])
        da = da + dk * x["kp"] * par[2:3]
        g1 = jnp.sum(dk * x["kp"] * (x["a"] - 1.0), 0, keepdims=True)
        dunit = x["inv"] * (dkk - x["kk"] * head_sum(dkk * x["kk"], ones))
        dkp = dkp + dunit * par[1:2]
        g0 = jnp.sum(dunit * x["kp"], 0, keepdims=True)
        dev = dv * (x["vf"] - x["vp"]) * x["s"] * (1.0 - x["s"])
        dea = da * x["a"] * (1.0 - x["a"])
        dew = dld * (-DECAY_SCALE) * x["sg"] * (1.0 - x["sg"])
        dr_ref[:, cols[p]] = dr.astype(BF)
        dkp_ref[:, cols[p]] = dkp.astype(BF)
        dvp_ref[:, cols[p]] = (dv * (1.0 - x["s"])).astype(BF)
        dvf_ref[:, cols[p]] = dv * x["s"]
        dew_ref[:, cols[p]] = dew.astype(BF)
        dea_ref[:, cols[p]] = dea.astype(BF)
        dev_ref[:, cols[p]] = dev.astype(BF)
        dpar_ref[:, cols[p]] += jnp.concatenate(
            [
                jnp.sum(dew, 0, keepdims=True),
                g0,
                g1,
                x["g2"],
                jnp.sum(dea, 0, keepdims=True),
                jnp.sum(dev, 0, keepdims=True),
                x["b2"],
                x["b3"],
            ],
            0,
        )


def token_spec(cols, order):
    return pl.BlockSpec((CHUNK, cols), lambda i: (order(i), 0))


def square_spec(pairs, order):
    return pl.BlockSpec((1, pairs, PAIR, PAIR), lambda i: (order(i), 0, 0, 0))


def mixer_forward(r, kp, vp, ew, ea, ev, gate, vf, par, gcol, aux):
    tokens, cols = r.shape
    steps, pairs = tokens // CHUNK, cols // PAIR
    order = lambda i: i
    tok = token_spec(cols, order)
    sq = square_spec(pairs, order)
    sq_shape = jax.ShapeDtypeStruct((steps, pairs, PAIR, PAIR), F32)
    tok_shape = jax.ShapeDtypeStruct((tokens, cols), F32)
    flops = steps * pairs * 19 * 3 * 2 * PAIR**3
    return pl.pallas_call(
        forward_kernel,
        name="mixer_forward",
        grid=(steps,),
        in_specs=[tok] * 8
        + [
            pl.BlockSpec((8, cols), lambda i: (0, 0)),
            pl.BlockSpec((CHUNK, 1), lambda i: (i, 0)),
            pl.BlockSpec((1, 8, PAIR), lambda i: (i, 0, 0)),
        ],
        out_specs=[tok, tok, tok] + [sq] * 5,
        out_shape=[jax.ShapeDtypeStruct((tokens, cols), BF), tok_shape, tok_shape] + [sq_shape] * 5,
        scratch_shapes=[pltpu.VMEM((pairs, PAIR, PAIR), F32)],
        compiler_params=pltpu.CompilerParams(vmem_limit_bytes=48 << 20),
        cost_estimate=pl.CostEstimate(flops=flops, bytes_accessed=22 << 20, transcendentals=8 * tokens * cols),
    )(r, kp, vp, ew, ea, ev, gate, vf, par, gcol, aux)


def mixer_backward(dz, r, kp, vp, ew, ea, ev, gate, vf, par, gcol, aux, y, q, t, akk, ark, arb, s0):
    tokens, cols = r.shape
    steps, pairs = tokens // CHUNK, cols // PAIR
    order = lambda i: steps - 1 - i
    tok = token_spec(cols, order)
    sq = square_spec(pairs, order)
    low = jax.ShapeDtypeStruct((tokens, cols), BF)
    flops = steps * pairs * 15 * 3 * 2 * PAIR**3
    return pl.pallas_call(
        backward_kernel,
        name="mixer_backward",
        grid=(steps,),
        in_specs=[tok] * 9
        + [
            pl.BlockSpec((8, cols), lambda i: (0, 0)),
            pl.BlockSpec((CHUNK, 1), lambda i: (order(i), 0)),
            pl.BlockSpec((1, 8, PAIR), lambda i: (order(i), 0, 0)),
        ]
        + [tok, tok]
        + [sq] * 5,
        out_specs=[tok] * 8 + [pl.BlockSpec((8, cols), lambda i: (0, 0))],
        out_shape=[low] * 7
        + [jax.ShapeDtypeStruct((tokens, cols), F32), jax.ShapeDtypeStruct((8, cols), F32)],
        scratch_shapes=[pltpu.VMEM((pairs, PAIR, PAIR), F32)],
        compiler_params=pltpu.CompilerParams(vmem_limit_bytes=48 << 20),
        cost_estimate=pl.CostEstimate(flops=flops, bytes_accessed=28 << 20, transcendentals=8 * tokens * cols),
    )(dz, r, kp, vp, ew, ea, ev, gate, vf, par, gcol, aux, y, q, t, akk, ark, arb, s0)


def document_tables(segments):
    rows, length = segments.shape
    marks = segments + (length + 1) * lax.broadcasted_iota(jnp.int32, (rows, length), 0)
    flat = marks.reshape(-1).astype(F32)
    blocks = flat.reshape(-1, CHUNK)
    ends = blocks[:, -1]
    before = jnp.concatenate([jnp.full((1,), -1.0, F32), ends[:-1]])
    wide = lambda x: jnp.broadcast_to(x[:, None], (x.shape[0], PAIR))
    aux = jnp.stack([jnp.concatenate([blocks, blocks], 1), wide(ends), wide(before)] + [jnp.zeros((blocks.shape[0], PAIR), F32)] * 5, 1)
    return flat[:, None], aux


def on_device(
    block_input,
    first_layer_values,
    segments,
    valid,
    cotangent,
    teacher,
    layer_norm_gain,
    layer_norm_bias,
    lerps,
    decay_offset,
    head_gain_table,
    per_unit_shift_array,
    lowrank_first_maps,
    lowrank_second_maps,
    receptance_key_value_weight,
    time_output_weight,
    channel_key_weight,
    channel_value_weight,
):
    tensor_size = lax.axis_size("tensor")
    tensor_pos = lax.axis_index("tensor")
    dp_pos = lax.axis_index("dp")
    own_rows = block_input.shape[0]
    model_width = block_input.shape[1]
    local_columns = receptance_key_value_weight.shape[2]
    column_begin = tensor_pos * local_columns
    row_begin = tensor_pos * own_rows
    divide_pair = DECAY_MAP_RANK + RATE_MAP_RANK
    divide_three = divide_pair + VALUE_MIX_RANK
    valid_rows = valid.astype(jnp.float32).reshape(-1)
    valid_token_count = jnp.sum(valid_rows)
    valid_own = lax.dynamic_slice_in_dim(
        valid_rows, (dp_pos * tensor_size + tensor_pos) * own_rows, own_rows
    )
    same_doc = (segments[:, 1:] == segments[:, :-1]).astype(jnp.float32)
    retain_mask = jnp.concatenate(
        [jnp.zeros((segments.shape[0], 1), jnp.float32), same_doc], 1
    ).reshape(-1)
    rkv_full, out_full, key_full, value_full = (
        lax.all_gather(receptance_key_value_weight, "dp", axis=1, tiled=True),
        lax.all_gather(time_output_weight, "dp", axis=1, tiled=True),
        lax.all_gather(channel_key_weight, "dp", axis=0, tiled=True),
        lax.all_gather(channel_value_weight, "dp", axis=1, tiled=True),
    )
    block_row_slice = block_input.astype(jnp.float32)
    normed_one, norm_one_back = jax.vjp(
        layer_norm, block_row_slice, layer_norm_gain[0], layer_norm_bias[0]
    )
    gathered = lax.all_gather(normed_one.astype(jnp.bfloat16), "tensor", axis=0, tiled=True).astype(
        jnp.float32
    )
    delta_one = shift_down(gathered, retain_mask) - gathered
    blended = [
        (gathered + delta_one * lerps[lane_index]).astype(jnp.bfloat16) for lane_index in range(6)
    ]
    acceptance_vector_lines = matrix_multiply(blended[0], rkv_full[0])
    key_projected = matrix_multiply(blended[2], rkv_full[1])
    value_projected = matrix_multiply(blended[3], rkv_full[2])
    decay_squashed = jnp.tanh(matrix_multiply(blended[1], lowrank_first_maps[:, :DECAY_MAP_RANK]))
    decay_inner = decay_squashed.astype(jnp.bfloat16)
    rate_inner = matrix_multiply(
        blended[4], lowrank_first_maps[:, DECAY_MAP_RANK:divide_pair]
    ).astype(jnp.bfloat16)
    value_inner = matrix_multiply(
        blended[3], lowrank_first_maps[:, divide_pair:divide_three]
    ).astype(jnp.bfloat16)
    gate_squashed = jax.nn.sigmoid(
        matrix_multiply(blended[5], lowrank_first_maps[:, divide_three:])
    )
    gate_inner = gate_squashed.astype(jnp.bfloat16)
    upper_columns = lax.dynamic_slice_in_dim(lowrank_second_maps, column_begin, local_columns, 1)
    decay_lowrank = matrix_multiply(decay_inner, upper_columns[:DECAY_MAP_RANK])
    rate_lowrank = matrix_multiply(rate_inner, upper_columns[DECAY_MAP_RANK:divide_pair])
    value_lowrank = matrix_multiply(value_inner, upper_columns[divide_pair:divide_three])
    output_switch_thin_factors = matrix_multiply(gate_inner, upper_columns[divide_three:])
    base_cols = lax.dynamic_slice_in_dim(decay_offset, column_begin, local_columns, 0)
    gain_cols = lax.dynamic_slice_in_dim(head_gain_table, column_begin, local_columns, 1)
    bias_cols = lax.dynamic_slice_in_dim(per_unit_shift_array, column_begin, local_columns, 1)
    par = jnp.concatenate([base_cols[None], gain_cols, bias_cols], 0)
    doc_col, doc_aux = document_tables(segments)
    mixer_low, *kept = mixer_forward(
        acceptance_vector_lines,
        key_projected,
        value_projected,
        decay_lowrank,
        rate_lowrank,
        value_lowrank,
        output_switch_thin_factors,
        first_layer_values,
        par,
        doc_col,
        doc_aux,
    )
    attended = lax.psum_scatter(
        matrix_multiply(mixer_low, out_full), "tensor", scatter_dimension=0, tiled=True
    )
    after_mixer = block_row_slice + attended
    normed_two, norm_two_back = jax.vjp(
        layer_norm, after_mixer, layer_norm_gain[1], layer_norm_bias[1]
    )
    gathered_two = lax.all_gather(
        normed_two.astype(jnp.bfloat16), "tensor", axis=0, tiled=True
    ).astype(jnp.float32)
    delta_two = shift_down(gathered_two, retain_mask) - gathered_two
    channel_in = (gathered_two + delta_two * lerps[6]).astype(jnp.bfloat16)
    channel_pre = matrix_multiply(channel_in, key_full)
    rectified = jnp.maximum(channel_pre, 0.0)
    hidden_low = (rectified * rectified).astype(jnp.bfloat16)
    channel = lax.psum_scatter(
        matrix_multiply(hidden_low, value_full), "tensor", scatter_dimension=0, tiled=True
    )
    block_sum = after_mixer + channel
    mismatch = block_sum - teacher.astype(jnp.float32)
    loss_part = jnp.sum(valid_own[:, None] * mismatch * mismatch) / (
        valid_token_count * model_width
    )
    seed = valid_own[:, None] * (
        cotangent.astype(jnp.float32) + 2.0 * mismatch / (valid_token_count * model_width)
    )
    seed_all = lax.all_gather(seed.astype(jnp.bfloat16), "tensor", axis=0, tiled=True)
    grad_value_part = matmul_tn(hidden_low, seed_all)
    hidden_grad = matrix_multiply_transposed(seed_all, value_full)
    pre_grad = (hidden_grad * 2.0 * rectified).astype(jnp.bfloat16)
    grad_key_part = matmul_tn(channel_in, pre_grad)
    channel_grad = matrix_multiply_transposed(pre_grad, key_full)
    lerp_six = jnp.sum(channel_grad * delta_two, 0)
    spread_two = channel_grad * (1.0 - lerps[6]) + shift_up(channel_grad * lerps[6], retain_mask)
    normed_two_grad = lax.psum_scatter(spread_two, "tensor", scatter_dimension=0, tiled=True)
    mixer_sum_grad, gain_two, bias_two = norm_two_back(normed_two_grad)
    after_grad = seed + mixer_sum_grad
    attended_all = lax.all_gather(after_grad.astype(jnp.bfloat16), "tensor", axis=0, tiled=True)
    grad_out_part = matmul_tn(mixer_low, attended_all)
    mixer_grad = matrix_multiply_transposed(attended_all, out_full)
    (
        recept_low,
        key_low,
        value_low,
        decay_low,
        rate_low,
        vlora_low,
        gate_low,
        first_grad,
        par_grad,
    ) = mixer_backward(
        mixer_grad,
        acceptance_vector_lines,
        key_projected,
        value_projected,
        decay_lowrank,
        rate_lowrank,
        value_lowrank,
        output_switch_thin_factors,
        first_layer_values,
        par,
        doc_col,
        doc_aux,
        *kept,
    )
    base_grad, gain_grad, bias_grad = par_grad[0], par_grad[1:4], par_grad[4:8]
    grad_rkv_part = jnp.stack(
        [
            matmul_tn(blended[0], recept_low),
            matmul_tn(blended[2], key_low),
            matmul_tn(blended[3], value_low),
        ]
    )
    grad_up_cols = jnp.concatenate(
        [
            matmul_tn(decay_inner, decay_low),
            matmul_tn(rate_inner, rate_low),
            matmul_tn(value_inner, vlora_low),
            matmul_tn(gate_inner, gate_low),
        ],
        0,
    )
    hidden_grads = jnp.concatenate(
        [
            matrix_multiply_transposed(decay_low, upper_columns[:DECAY_MAP_RANK])
            * (1.0 - decay_squashed * decay_squashed),
            matrix_multiply_transposed(rate_low, upper_columns[DECAY_MAP_RANK:divide_pair]),
            matrix_multiply_transposed(vlora_low, upper_columns[divide_pair:divide_three]),
            matrix_multiply_transposed(gate_low, upper_columns[divide_three:])
            * gate_squashed
            * (1.0 - gate_squashed),
        ],
        1,
    )
    hidden_local = lax.psum_scatter(hidden_grads, "tensor", scatter_dimension=0, tiled=True).astype(
        jnp.bfloat16
    )
    own_mixed = [
        lax.dynamic_slice_in_dim(blended[lane_index], row_begin, own_rows, 0)
        for lane_index in (1, 4, 3, 5)
    ]
    grad_down = jnp.concatenate(
        [
            matmul_tn(own_mixed[0], hidden_local[:, :DECAY_MAP_RANK]),
            matmul_tn(own_mixed[1], hidden_local[:, DECAY_MAP_RANK:divide_pair]),
            matmul_tn(own_mixed[2], hidden_local[:, divide_pair:divide_three]),
            matmul_tn(own_mixed[3], hidden_local[:, divide_three:]),
        ],
        1,
    )
    blank_rows = jnp.zeros(gathered.shape, jnp.float32)
    mixed_grads = [
        matrix_multiply_transposed(recept_low, rkv_full[0]),
        add_rows(
            blank_rows,
            matrix_multiply_transposed(
                hidden_local[:, :DECAY_MAP_RANK], lowrank_first_maps[:, :DECAY_MAP_RANK]
            ),
            row_begin,
        ),
        matrix_multiply_transposed(key_low, rkv_full[1]),
        add_rows(
            matrix_multiply_transposed(value_low, rkv_full[2]),
            matrix_multiply_transposed(
                hidden_local[:, divide_pair:divide_three],
                lowrank_first_maps[:, divide_pair:divide_three],
            ),
            row_begin,
        ),
        add_rows(
            blank_rows,
            matrix_multiply_transposed(
                hidden_local[:, DECAY_MAP_RANK:divide_pair],
                lowrank_first_maps[:, DECAY_MAP_RANK:divide_pair],
            ),
            row_begin,
        ),
        add_rows(
            blank_rows,
            matrix_multiply_transposed(
                hidden_local[:, divide_three:], lowrank_first_maps[:, divide_three:]
            ),
            row_begin,
        ),
    ]
    spread_one = blank_rows
    carried = blank_rows
    lerp_rows = []
    for lane_index in range(6):
        lane_grad = mixed_grads[lane_index]
        lerp_rows.append(jnp.sum(lane_grad * delta_one, 0))
        spread_one = spread_one + lane_grad * (1.0 - lerps[lane_index])
        carried = carried + lane_grad * lerps[lane_index]
    spread_one = spread_one + shift_up(carried, retain_mask)
    normed_one_grad = lax.psum_scatter(spread_one, "tensor", scatter_dimension=0, tiled=True)
    input_grad, gain_one, bias_one = norm_one_back(normed_one_grad)
    grad_in = after_grad + input_grad
    small_terms = (
        jnp.stack([gain_one, gain_two]),
        jnp.stack([bias_one, bias_two]),
        jnp.stack(lerp_rows + [lerp_six]),
        place_cols(base_grad, model_width, column_begin),
        place_cols(gain_grad, model_width, column_begin),
        place_cols(bias_grad, model_width, column_begin),
        grad_down,
        place_cols(grad_up_cols, model_width, column_begin),
        loss_part,
    )
    summed = lax.psum(
        (
            small_terms[0],
            small_terms[1],
            small_terms[2],
            small_terms[3],
            small_terms[4],
            small_terms[5],
            small_terms[6],
            small_terms[7],
            small_terms[8],
        ),
        ("dp", "tensor"),
    )
    grad_rkv, grad_out_weight, grad_key_weight, grad_value_weight = (
        lax.psum_scatter(grad_rkv_part, "dp", scatter_dimension=1, tiled=True),
        lax.psum_scatter(grad_out_part, "dp", scatter_dimension=1, tiled=True),
        lax.psum_scatter(grad_key_part, "dp", scatter_dimension=0, tiled=True),
        lax.psum_scatter(grad_value_part, "dp", scatter_dimension=1, tiled=True),
    )
    lerp_summed = summed[2]
    return (
        block_sum.astype(jnp.bfloat16),
        summed[8],
        grad_in,
        first_grad,
        summed[0],
        summed[1],
        jnp.concatenate([lerp_summed[:1], lerp_summed[2:]], 0),
        lerp_summed[1],
        summed[3],
        summed[4],
        summed[5],
        summed[6],
        summed[7],
        grad_rkv,
        grad_out_weight,
        grad_key_weight,
        grad_value_weight,
    )


def solution(mesh):
    return jax.shard_map(
        on_device,
        mesh=mesh,
        in_specs=(
            P(("dp", "tensor"), None),
            P("dp", "tensor"),
            P("dp", None),
            P(),
            P(("dp", "tensor"), None),
            P(("dp", "tensor"), None),
            P(),
            P(),
            P(),
            P(),
            P(),
            P(),
            P(),
            P(),
            P(None, "dp", "tensor"),
            P("tensor", "dp"),
            P("dp", "tensor"),
            P("tensor", "dp"),
        ),
        out_specs=(
            P(("dp", "tensor"), None),
            P(),
            P(("dp", "tensor"), None),
            P("dp", "tensor"),
            P(),
            P(),
            P(),
            P(),
            P(),
            P(),
            P(),
            P(),
            P(),
            P(None, "dp", "tensor"),
            P("tensor", "dp"),
            P("dp", "tensor"),
            P("tensor", "dp"),
        ),
        check_vma=False,
    )
```

```python
import jax
import jax.numpy as jnp
from jax import lax
from jax.experimental import pallas as pl
from jax.experimental.pallas import tpu as pltpu
from jax.sharding import PartitionSpec as P

HEAD_SIZE = 64
CHUNK = 64
PAIR = 2 * HEAD_SIZE
BF = jnp.bfloat16
F32 = jnp.float32
DECAY_SCALE = 0.6065306597126334
DECAY_MAP_RANK = 64
RATE_MAP_RANK = 64
VALUE_MIX_RANK = 32


def matrix_multiply(left, right):
    return jnp.dot(left, right, preferred_element_type=jnp.float32)


def matmul_tn(left, right):
    return lax.dot_general(
        left, right, (((0,), (0,)), ((), ())), preferred_element_type=jnp.float32
    )


def matrix_multiply_transposed(left, right):
    return lax.dot_general(
        left, right, (((1,), (1,)), ((), ())), preferred_element_type=jnp.float32
    )


def shift_down(row_data, retain_mask):
    return jnp.concatenate([jnp.zeros_like(row_data[:1]), row_data[:-1]], 0) * retain_mask[:, None]


def shift_up(row_data, retain_mask):
    moved = row_data * retain_mask[:, None]
    return jnp.concatenate([moved[1:], jnp.zeros_like(moved[:1])], 0)


def place_cols(col_block, total_cols, first_col):
    zeros_full = jnp.zeros(col_block.shape[:-1] + (total_cols,), jnp.float32)
    return lax.dynamic_update_slice_in_dim(zeros_full, col_block, first_col, col_block.ndim - 1)


NN = (((1,), (0,)), ((), ()))
NT = (((1,), (1,)), ((), ()))
TN = (((0,), (0,)), ((), ()))


def split(x, terms=2):
    hi = x.astype(BF)
    if terms == 1:
        return (hi,)
    return (hi, (x - hi.astype(F32)).astype(BF))


def mm(a, b, dims):
    out = lax.dot_general(a[0], b[0], dims, preferred_element_type=F32)
    if len(b) > 1:
        out = out + lax.dot_general(a[0], b[1], dims, preferred_element_type=F32)
    if len(a) > 1:
        out = out + lax.dot_general(a[1], b[0], dims, preferred_element_type=F32)
    return out


def rows_of(*parts):
    return tuple(jnp.concatenate(terms, 0) for terms in zip(*parts))


def cols_of(*parts):
    return tuple(jnp.concatenate(terms, 1) for terms in zip(*parts))


def spread(parts, left, right):
    return tuple(jnp.concatenate([x * left, x * right], 0) for x in parts)


def chunk_masks(gcol, aux):
    size = 2 * CHUNK
    row = lax.broadcasted_iota(jnp.int32, (size, size), 0)
    lane = lax.broadcasted_iota(jnp.int32, (size, size), 1)
    t_row, t_lane = row & (CHUNK - 1), lane & (CHUNK - 1)
    same_head = (row >= CHUNK) == (lane >= CHUNK)
    g_row = jnp.concatenate([gcol, gcol], 0)
    linked = (g_row == aux[0:1, :]) & same_head
    strict = linked & (t_row > t_lane)
    upto = linked & (t_row >= t_lane)
    from_start = (gcol == aux[2:3, :]).astype(F32)
    to_end = (gcol == aux[1:2, :]).astype(F32)
    end_clear = (aux[1:2, :] == aux[2:3, :]).astype(F32)
    return row, lane, t_row, t_lane, strict, upto, from_start, to_end, end_clear


def head_sum(x, ones):
    return mm(split(x), (ones,), NN)


def lane_masks():
    lane = lax.broadcasted_iota(jnp.int32, (1, PAIR), 1)
    left = (lane < HEAD_SIZE).astype(F32)
    return left.astype(BF), (1.0 - left).astype(BF), left


def head_ones():
    row = lax.broadcasted_iota(jnp.int32, (PAIR, PAIR), 0)
    lane = lax.broadcasted_iota(jnp.int32, (PAIR, PAIR), 1)
    return ((row >= HEAD_SIZE) == (lane >= HEAD_SIZE)).astype(F32).astype(BF)


def lower_ones():
    row = lax.broadcasted_iota(jnp.int32, (CHUNK, CHUNK), 0)
    lane = lax.broadcasted_iota(jnp.int32, (CHUNK, CHUNK), 1)
    return (row >= lane).astype(F32).astype(BF)


def split3(x):
    hi = x.astype(BF)
    rest = x - hi.astype(F32)
    mid = rest.astype(BF)
    return (hi, mid, (rest - mid.astype(F32)).astype(BF))


def ones_times(ones, x, dims):
    total = None
    for term in split3(x):
        part = lax.dot_general(ones, term, dims, preferred_element_type=F32)
        total = part if total is None else total + part
    return total


def sigmoid(x):
    return jax.nn.sigmoid(x)


def low_cols(ref, index, cols):
    start = index * (ref.shape[1] // 4)
    return slice(start + cols.start, start + cols.stop)


def pair_values(refs, par, cols, ones):
    r_ref, kp_ref, vp_ref, low_ref, vf_ref = refs
    out = {}
    r, kp, vp = r_ref[:, cols], kp_ref[:, cols], vp_ref[:, cols]
    vf = vf_ref[:, cols].astype(F32)
    a = sigmoid(par[4:5] + low_ref[:, low_cols(low_ref, 1, cols)])
    s = sigmoid(par[5:6] + low_ref[:, low_cols(low_ref, 2, cols)])
    v = vp + (vf - vp) * s
    sg = sigmoid(par[0:1] + low_ref[:, low_cols(low_ref, 0, cols)])
    ld = -DECAY_SCALE * sg
    u = kp * par[1:2]
    inv = lax.rsqrt(head_sum(u * u, ones) + 1e-06)
    kk = u * inv
    k = kp * (1.0 + (a - 1.0) * par[2:3])
    out.update(r=r, kp=kp, vp=vp, vf=vf, a=a, s=s, v=v, sg=sg, ld=ld, inv=inv, kk=kk, k=k)
    return out


def chunk_values(w, lower, from_start, to_end, end_clear):
    inc = ones_times(lower, w["ld"], NN)
    exc = inc - w["ld"]
    last = inc[CHUNK - 1 : CHUNK, :]
    w["e_inc"] = jnp.exp(inc)
    w["e_exc"] = jnp.exp(exc)
    w["e_neg"] = jnp.exp(-inc)
    w["carry"] = jnp.exp(last - inc) * to_end
    w["finish"] = jnp.exp(last) * end_clear
    w["b"] = w["kk"] * w["a"]
    w["kappa"] = w["kk"] * w["e_exc"]
    w["rho"] = w["r"] * w["e_inc"]
    w["key_hat"] = w["k"] * w["e_neg"]
    w["take_hat"] = w["b"] * w["e_neg"]
    w["k_end"] = w["k"] * w["carry"]
    w["b_end"] = w["b"] * w["carry"]
    w["kappa0"] = w["kappa"] * from_start
    w["rho0"] = w["rho"] * from_start


def forward_kernel(
    r_ref, kp_ref, vp_ref, low_ref, vf_ref, par_ref, gcol_ref, aux_ref,
    z_ref, y_ref, q_ref, t_ref, akk_ref, ark_ref, arb_ref, s0_ref, state,
):
    pairs = r_ref.shape[1] // PAIR

    @pl.when(pl.program_id(0) == 0)
    def _():
        state[...] = jnp.zeros_like(state)

    masks = chunk_masks(gcol_ref[...], aux_ref[0])
    row, lane, t_row, t_lane, strict, upto, from_start, to_end, end_clear = masks
    left, right, left_f = lane_masks()
    ones = head_ones()
    lower = lower_ones()
    eye = (row == lane).astype(F32)
    in8 = (t_row >> 3) == (t_lane >> 3)
    levels = []
    for bits in (3, 4, 5):
        levels.append(((t_row >> (bits + 1)) == (t_lane >> (bits + 1))) & ((t_row >> bits) != (t_lane >> bits)))
    group = range(pairs)
    cols = [slice(p * PAIR, (p + 1) * PAIR) for p in group]
    refs = (r_ref, kp_ref, vp_ref, low_ref, vf_ref)
    pars = [par_ref[:, cols[p]] for p in group]
    w = [pair_values(refs, pars[p], cols[p], ones) for p in group]
    for p in group:
        chunk_values(w[p], lower, from_start, to_end, end_clear)
    akk, akb, ark, arb = [], [], [], []
    for p in group:
        x = w[p]
        rows = rows_of(spread(split(x["kappa"]), left, right), spread(split(x["rho"]), left, right))
        keys = rows_of(spread(split(x["key_hat"]), left, right), spread(split(x["take_hat"]), left, right))
        scores = mm(rows, keys, NT)
        n = 2 * CHUNK
        akk.append(jnp.where(strict, scores[:n, :n], 0.0))
        akb.append(jnp.where(strict, scores[:n, n:], 0.0))
        ark.append(jnp.where(upto, scores[n:, :n], 0.0))
        arb.append(jnp.where(upto, scores[n:, n:], 0.0))
    neg = [jnp.where(in8, -akb[p], 0.0) for p in group]
    neg_s = [split(x) for x in neg]
    two = [mm(x, x, NN) for x in neg_s]
    two_s = [split(x) for x in two]
    both = [mm(rows_of(neg_s[p], two_s[p]), two_s[p], NN) for p in group]
    n = 2 * CHUNK
    low = [neg[p] + two[p] + both[p][:n] for p in group]
    four = [both[p][n:] for p in group]
    inv = [eye + low[p] + four[p] + mm(split(low[p]), split(four[p]), NN) for p in group]
    for level in levels:
        inv_s = [split(x) for x in inv]
        mid = [mm(split(jnp.where(level, akb[p], 0.0)), inv_s[p], NN) for p in group]
        inv = [inv[p] - mm(inv_s[p], split(mid[p]), NN) for p in group]
    inv_s = [split(x) for x in inv]
    v_s = [spread(split(w[p]["v"]), left, right) for p in group]
    akk_v = [mm(split(akk[p]), v_s[p], NN) for p in group]
    s0 = [state[p] for p in group]
    carried = [
        mm(
            rows_of(spread(split(w[p]["kappa0"]), left, right), spread(split(w[p]["rho0"]), left, right)),
            split(s0[p]),
            NT,
        )
        for p in group
    ]
    q = [mm(inv_s[p], split(carried[p][:n] + akk_v[p]), NN) for p in group]
    q_s = [split(x) for x in q]
    y2 = [
        carried[p][n:] + mm(cols_of(split(ark[p]), split(-arb[p])), rows_of(v_s[p], q_s[p]), NN)
        for p in group
    ]
    for p in group:
        x = w[p]
        ends = rows_of(spread(split(x["k_end"]), left, right), spread(split(-x["b_end"]), left, right))
        state[p] = s0[p] * x["finish"] + mm(rows_of(v_s[p], q_s[p]), ends, TN)
        y = y2[p][:CHUNK] + y2[p][CHUNK:]
        y_ref[:, cols[p]] = y
        q_ref[:, cols[p]] = q[p][:CHUNK] + q[p][CHUNK:]
        t_ref[0, p] = inv[p]
        akk_ref[0, p] = akk[p]
        ark_ref[0, p] = ark[p]
        arb_ref[0, p] = arb[p]
        s0_ref[0, p] = s0[p]
        par = pars[p]
        centred = y - head_sum(y, ones) * (1.0 / HEAD_SIZE)
        var = head_sum(centred * centred, ones) * (1.0 / HEAD_SIZE)
        normed = centred * lax.rsqrt(var + HEAD_SIZE * 0.01)
        bonus = head_sum(x["r"] * x["k"] * par[6:7], ones)
        z = (normed * par[3:4] + par[7:8] + bonus * x["v"]) * low_ref[:, low_cols(low_ref, 3, cols[p])]
        z_ref[:, cols[p]] = z.astype(z_ref.dtype)


def backward_kernel(
    dz_ref, r_ref, kp_ref, vp_ref, low_ref, vf_ref, par_ref, gcol_ref, aux_ref,
    y_ref, q_ref, t_ref, akk_ref, ark_ref, arb_ref, s0_ref,
    dr_ref, dkp_ref, dvp_ref, dlow_ref, dvf_ref, dpar_ref, state,
):
    pairs = r_ref.shape[1] // PAIR
    n = 2 * CHUNK

    @pl.when(pl.program_id(0) == 0)
    def _():
        state[...] = jnp.zeros_like(state)
        dpar_ref[...] = jnp.zeros_like(dpar_ref)

    masks = chunk_masks(gcol_ref[...], aux_ref[0])
    row, lane, t_row, t_lane, strict, upto, from_start, to_end, end_clear = masks
    left, right, left_f = lane_masks()
    ones = head_ones()
    lower = lower_ones()
    last_row = (lax.broadcasted_iota(jnp.int32, (CHUNK, 1), 0) == CHUNK - 1).astype(F32)
    group = range(pairs)
    cols = [slice(p * PAIR, (p + 1) * PAIR) for p in group]
    refs = (r_ref, kp_ref, vp_ref, low_ref, vf_ref)
    pars = [par_ref[:, cols[p]] for p in group]
    w = [pair_values(refs, pars[p], cols[p], ones) for p in group]
    scale = 1.0 / HEAD_SIZE
    for p in group:
        x, par = w[p], pars[p]
        chunk_values(x, lower, from_start, to_end, end_clear)
        y = y_ref[:, cols[p]]
        centred = y - head_sum(y, ones) * scale
        var = head_sum(centred * centred, ones) * scale
        istd = lax.rsqrt(var + HEAD_SIZE * 0.01)
        normed = centred * istd
        rk = x["r"] * x["k"]
        bonus = head_sum(rk * par[6:7], ones)
        dz = dz_ref[:, cols[p]]
        dlow_ref[:, low_cols(low_ref, 3, cols[p])] = (dz * (normed * par[3:4] + par[7:8] + bonus * x["v"])).astype(BF)
        do = dz * low_ref[:, low_cols(low_ref, 3, cols[p])]
        dbonus = head_sum(do * x["v"], ones)
        x["dv"] = do * bonus
        x["dr"] = dbonus * x["k"] * par[6:7]
        x["dk"] = dbonus * x["r"] * par[6:7]
        dn = do * par[3:4]
        x["dy"] = istd * (dn - head_sum(dn, ones) * scale - normed * (head_sum(dn * normed, ones) * scale))
        x["g2"] = jnp.sum(do * normed, 0, keepdims=True)
        x["b3"] = jnp.sum(do, 0, keepdims=True)
        x["b2"] = jnp.sum(dbonus * rk, 0, keepdims=True)
    dy_s = [spread(split(w[p]["dy"]), left, right) for p in group]
    v_s = [spread(split(w[p]["v"]), left, right) for p in group]
    q_s = [spread(split(q_ref[:, cols[p]]), left, right) for p in group]
    ds = [state[p] for p in group]
    ds_s = [split(ds[p]) for p in group]
    kend_s = [spread(split(w[p]["k_end"]), left, right) for p in group]
    bend_s = [spread(split(w[p]["b_end"]), left, right) for p in group]
    from_end = [mm(rows_of(kend_s[p], bend_s[p]), ds_s[p], NT) for p in group]
    dq = [-(mm(split(arb_ref[0, p]), dy_s[p], TN) + from_end[p][n:]) for p in group]
    du = [mm(split(t_ref[0, p]), split(dq[p]), TN) for p in group]
    du_s = [split(du[p]) for p in group]
    uy_s = [rows_of(du_s[p], dy_s[p]) for p in group]
    s0 = [s0_ref[0, p] for p in group]
    kappa_s = [spread(split(w[p]["kappa"]), left, right) for p in group]
    rho_s = [spread(split(w[p]["rho"]), left, right) for p in group]
    for p in group:
        x = w[p]
        start = rows_of(spread(split(x["kappa0"]), left, right), spread(split(x["rho0"]), left, right))
        state[p] = ds[p] * x["finish"] + mm(uy_s[p], start, TN)
    dv2 = [
        from_end[p][:n] + mm(rows_of(split(akk_ref[0, p]), split(ark_ref[0, p])), uy_s[p], TN)
        for p in group
    ]
    start_grad = [mm(uy_s[p], split(s0[p]), NN) for p in group]
    end_grad = [mm(rows_of(v_s[p], q_s[p]), ds_s[p], NN) for p in group]
    vq_s = [rows_of(v_s[p], tuple(-t for t in q_s[p])) for p in group]
    raw = [mm(uy_s[p], vq_s[p], NT) for p in group]
    da_s = []
    for p in group:
        top = jnp.where(jnp.concatenate([strict, strict], 1), raw[p][:n], 0.0)
        bottom = jnp.where(jnp.concatenate([upto, upto], 1), raw[p][n:], 0.0)
        da_s.append(split(jnp.concatenate([top, bottom], 0)))
    row_grad = [
        mm(
            da_s[p],
            rows_of(spread(split(w[p]["key_hat"]), left, right), spread(split(w[p]["take_hat"]), left, right)),
            NN,
        )
        for p in group
    ]
    col_grad = [mm(da_s[p], rows_of(kappa_s[p], rho_s[p]), TN) for p in group]

    def fold(z):
        return z[:CHUNK] + z[CHUNK:n], z[n : n + CHUNK] + z[n + CHUNK :]

    for p in group:
        x, par = w[p], pars[p]
        dkappa0, drho0 = fold(start_grad[p])
        dkend, dbend = fold(end_grad[p])
        dbend = -dbend
        dkappa, drho = fold(row_grad[p])
        dkey, dtake = fold(col_grad[p])
        dkappa = dkappa + dkappa0 * from_start
        drho = drho + drho0 * from_start
        dv = x["dv"] + dv2[p][:CHUNK] + dv2[p][CHUNK:]
        dr = x["dr"] + drho * x["e_inc"]
        dk = x["dk"] + dkey * x["e_neg"] + dkend * x["carry"]
        db = dtake * x["e_neg"] + dbend * x["carry"]
        dkk = dkappa * x["e_exc"] + db * x["a"]
        da = db * x["kk"]
        dexc = dkappa * x["kappa"]
        dends = dkend * x["k_end"] + dbend * x["b_end"]
        dinc = drho * x["rho"] - dkey * x["key_hat"] - dtake * x["take_hat"] - dends
        dlast = jnp.sum(dends, 0, keepdims=True) + jnp.sum(s0[p] * ds[p], 0, keepdims=True) * x["finish"]
        dld = ones_times(lower, dinc + dexc + last_row * dlast, TN) - dexc
        dkp = dk * (1.0 + (x["a"] - 1.0) * par[2:3])
        da = da + dk * x["kp"] * par[2:3]
        g1 = jnp.sum(dk * x["kp"] * (x["a"] - 1.0), 0, keepdims=True)
        dunit = x["inv"] * (dkk - x["kk"] * head_sum(dkk * x["kk"], ones))
        dkp = dkp + dunit * par[1:2]
        g0 = jnp.sum(dunit * x["kp"], 0, keepdims=True)
        dev = dv * (x["vf"] - x["vp"]) * x["s"] * (1.0 - x["s"])
        dea = da * x["a"] * (1.0 - x["a"])
        dew = dld * (-DECAY_SCALE) * x["sg"] * (1.0 - x["sg"])
        dr_ref[:, cols[p]] = dr.astype(BF)
        dkp_ref[:, cols[p]] = dkp.astype(BF)
        dvp_ref[:, cols[p]] = (dv * (1.0 - x["s"])).astype(BF)
        dvf_ref[:, cols[p]] = dv * x["s"]
        dlow_ref[:, low_cols(low_ref, 0, cols[p])] = dew.astype(BF)
        dlow_ref[:, low_cols(low_ref, 1, cols[p])] = dea.astype(BF)
        dlow_ref[:, low_cols(low_ref, 2, cols[p])] = dev.astype(BF)
        dpar_ref[:, cols[p]] += jnp.concatenate(
            [
                jnp.sum(dew, 0, keepdims=True),
                g0,
                g1,
                x["g2"],
                jnp.sum(dea, 0, keepdims=True),
                jnp.sum(dev, 0, keepdims=True),
                x["b2"],
                x["b3"],
            ],
            0,
        )


def token_spec(cols, order):
    return pl.BlockSpec((CHUNK, cols), lambda i: (order(i), 0))


def square_spec(pairs, order):
    return pl.BlockSpec((1, pairs, PAIR, PAIR), lambda i: (order(i), 0, 0, 0))


def mixer_specs(cols, order):
    tok = token_spec(cols, order)
    return [tok, tok, tok, token_spec(4 * cols, order), tok] + [
        pl.BlockSpec((8, cols), lambda i: (0, 0)),
        pl.BlockSpec((CHUNK, 1), lambda i: (order(i), 0)),
        pl.BlockSpec((1, 8, PAIR), lambda i: (order(i), 0, 0)),
    ]


def mixer_forward(r, *rest):
    tokens, cols = r.shape
    steps, pairs = tokens // CHUNK, cols // PAIR
    order = lambda i: i
    tok = token_spec(cols, order)
    sq = square_spec(pairs, order)
    sq_shape = jax.ShapeDtypeStruct((steps, pairs, PAIR, PAIR), F32)
    tok_shape = jax.ShapeDtypeStruct((tokens, cols), F32)
    return pl.pallas_call(
        forward_kernel,
        name="mixer_forward",
        grid=(steps,),
        in_specs=mixer_specs(cols, order),
        out_specs=[tok, tok, tok] + [sq] * 5,
        out_shape=[jax.ShapeDtypeStruct((tokens, cols), BF), tok_shape, tok_shape] + [sq_shape] * 5,
        scratch_shapes=[pltpu.VMEM((pairs, PAIR, PAIR), F32)],
        compiler_params=pltpu.CompilerParams(vmem_limit_bytes=48 << 20),
        cost_estimate=pl.CostEstimate(
            flops=steps * pairs * 600 * PAIR**3,
            bytes_accessed=22 << 20,
            transcendentals=8 * tokens * cols,
        ),
    )(r, *rest)


def mixer_backward(dz, r, *rest):
    tokens, cols = r.shape
    steps, pairs = tokens // CHUNK, cols // PAIR
    order = lambda i: steps - 1 - i
    tok = token_spec(cols, order)
    wide = token_spec(4 * cols, order)
    sq = square_spec(pairs, order)
    low = jax.ShapeDtypeStruct((tokens, cols), BF)
    return pl.pallas_call(
        backward_kernel,
        name="mixer_backward",
        grid=(steps,),
        in_specs=[tok] + mixer_specs(cols, order) + [tok, tok] + [sq] * 5,
        out_specs=[tok, tok, tok, wide, tok, pl.BlockSpec((8, cols), lambda i: (0, 0))],
        out_shape=[low] * 3
        + [
            jax.ShapeDtypeStruct((tokens, 4 * cols), BF),
            jax.ShapeDtypeStruct((tokens, cols), F32),
            jax.ShapeDtypeStruct((8, cols), F32),
        ],
        scratch_shapes=[pltpu.VMEM((pairs, PAIR, PAIR), F32)],
        compiler_params=pltpu.CompilerParams(vmem_limit_bytes=48 << 20),
        cost_estimate=pl.CostEstimate(
            flops=steps * pairs * 600 * PAIR**3,
            bytes_accessed=28 << 20,
            transcendentals=8 * tokens * cols,
        ),
    )(dz, r, *rest)


def part_masks(parts, total):
    lane = lax.broadcasted_iota(jnp.int32, (1, total), 1)
    return [((lane >= a) & (lane < b)).astype(F32).astype(BF) for a, b in parts]


def halves(value, own, rows):
    value = value.reshape(-1, 2, rows, value.shape[-1])
    flag = own == 1
    sent = jnp.where(flag, value[:, 0], value[:, 1])
    kept = jnp.where(flag, value[:, 1], value[:, 0])
    shape = (-1, value.shape[-1])
    return sent.reshape(shape).astype(BF), kept.reshape(shape).astype(BF)


def weight_grad_kernel(rows, sizes, own_ref, *refs):
    count = sum(sizes)
    left, right = refs[:count], refs[count : 2 * count]
    outs = refs[2 * count :]
    at = 0
    for i, size in enumerate(sizes):
        for k in range(size):
            value = lax.dot_general(left[at][...], right[at][...], TN, preferred_element_type=F32)
            sent, kept = halves(value, own_ref[0], rows)
            outs[2 * i][k] = sent
            outs[2 * i + 1][k] = kept
            at += 1


def weight_grads(own, rows, sizes, left, right):
    tokens, width = left[0].shape
    block = column_block(width)
    count = len(left)
    out_specs, out_shape, at = [], [], 0
    for size in sizes:
        cols = right[at].shape[1]
        at += size
        out_specs += [pl.BlockSpec((size, block // 2, cols), lambda j, own: (0, j, 0))] * 2
        out_shape += [jax.ShapeDtypeStruct((size, width // 2, cols), BF)] * 2
    out = pl.pallas_call(
        lambda *refs: weight_grad_kernel(rows, sizes, *refs),
        name="weight_grads",
        grid_spec=pltpu.PrefetchScalarGridSpec(
            num_scalar_prefetch=1,
            grid=(width // block,),
            in_specs=[pl.BlockSpec((tokens, block), lambda j, own: (0, j))] * count
            + [pl.BlockSpec((tokens, r.shape[1]), lambda j, own: (0, 0)) for r in right],
            out_specs=out_specs,
        ),
        out_shape=out_shape,
        compiler_params=pltpu.CompilerParams(vmem_limit_bytes=56 << 20),
        cost_estimate=pl.CostEstimate(
            flops=2 * tokens * width * sum(r.shape[1] for r in right),
            bytes_accessed=12 << 20,
            transcendentals=0,
        ),
    )(own, *left, *right)
    return [(out[2 * i], out[2 * i + 1]) for i in range(len(sizes))]


def channel_grad_kernel(key_left, key_right, value_left, value_right, out_ref):
    for i, (left, right) in enumerate(((key_left, key_right), (value_left, value_right))):
        out_ref[i] = lax.dot_general(
            left[...], right[...], TN, preferred_element_type=F32
        ).astype(BF)


def channel_grads(channel_in, pre_grad, seed, hidden):
    tokens, width = channel_in.shape
    units = hidden.shape[1]
    block = column_block(width)
    rows = pl.BlockSpec((tokens, block), lambda j: (0, j))
    full = pl.BlockSpec((tokens, units), lambda j: (0, 0))
    return pl.pallas_call(
        channel_grad_kernel,
        name="channel_grads",
        grid=(width // block,),
        in_specs=[rows, full, rows, full],
        out_specs=pl.BlockSpec((2, block, units), lambda j: (0, j, 0)),
        out_shape=jax.ShapeDtypeStruct((2, width, units), BF),
        compiler_params=pltpu.CompilerParams(vmem_limit_bytes=56 << 20),
        cost_estimate=pl.CostEstimate(
            flops=4 * tokens * width * units, bytes_accessed=14 << 20, transcendentals=0
        ),
    )(channel_in, pre_grad, seed, hidden)


def column_block(total):
    return 256 if total % 256 == 0 else 128


def input_grad_kernel(
    parts, x_ref, mean_ref, scale_ref, keep_ref, gain_ref, bias_ref, lerp_ref,
    gr_ref, gk_ref, gv_ref, wr_ref, wk_ref, wv_ref, hidden_ref, first_ref, spread_ref, sums_ref,
):
    tokens = x_ref.shape[0]
    unit = (x_ref[...].astype(F32) - mean_ref[...]) * scale_ref[...]
    normed = (unit * gain_ref[...] + bias_ref[...]).astype(BF).astype(F32)
    keep = keep_ref[...]
    delta = pltpu.roll(normed, 1, 0) * keep - normed
    hidden = hidden_ref[...]
    masks = part_masks(parts, hidden.shape[1])
    low = [
        lax.dot_general(hidden * masks[i], first_ref[...], NT, preferred_element_type=F32)
        for i in range(4)
    ]

    def back(g_ref, w_ref):
        return lax.dot_general(g_ref[...], w_ref[...], NT, preferred_element_type=F32)

    grads = [
        back(gr_ref, wr_ref), low[0], back(gk_ref, wk_ref), back(gv_ref, wv_ref) + low[2], low[1], low[3],
    ]
    total = grads[0]
    carried = grads[0] * lerp_ref[0:1]
    for i in range(1, 6):
        total = total + grads[i]
        carried = carried + grads[i] * lerp_ref[i : i + 1]
    spread_rows = total - carried + pltpu.roll(carried * keep, tokens - 1, 0)
    spread_ref[...] = spread_rows
    rows = [jnp.sum(g * delta, 0, keepdims=True) for g in grads]
    rows.append(jnp.sum(spread_rows * unit, 0, keepdims=True))
    rows.append(jnp.sum(spread_rows, 0, keepdims=True))
    sums_ref[...] = jnp.concatenate(rows, 0)


def input_grads(x, mean, scale, keep, gain, bias, lerps, grads, weights, hidden, first, parts):
    tokens, width = x.shape
    cols = grads[0].shape[1]
    ranks = hidden.shape[1]
    block = column_block(width)
    side = lambda n: pl.BlockSpec((tokens, n), lambda j: (0, 0))
    top = lambda n: pl.BlockSpec((n, block), lambda j: (0, j))
    wide = lambda n: pl.BlockSpec((block, n), lambda j: (j, 0))
    return pl.pallas_call(
        lambda *refs: input_grad_kernel(parts, *refs),
        name="input_grads",
        grid=(width // block,),
        in_specs=[top(tokens), side(1), side(1), side(1), top(1), top(1), top(6)]
        + [side(cols)] * 3
        + [wide(cols)] * 3
        + [side(ranks), wide(ranks)],
        out_specs=[top(tokens), top(8)],
        out_shape=[jax.ShapeDtypeStruct((tokens, width), F32), jax.ShapeDtypeStruct((8, width), F32)],
        compiler_params=pltpu.CompilerParams(vmem_limit_bytes=48 << 20),
        cost_estimate=pl.CostEstimate(
            flops=8 * tokens * width * cols, bytes_accessed=10 << 20, transcendentals=0
        ),
    )(x, mean, scale, keep, gain, bias, lerps, *grads, *weights, hidden, first)


def lowrank_grad_kernel(
    parts, groups, place_ref, m1_ref, m4_ref, m3_ref, m5_ref, hidden_ref,
    g0_ref, g1_ref, g2_ref, g3_ref, inner_ref, par_ref,
    first_down_ref, first_up_ref, second_down_ref, second_up_ref, out_ref,
):
    hidden, inner = hidden_ref[...], inner_ref[...]
    ranks = hidden.shape[1]
    masks = part_masks(parts, ranks)
    total = out_ref.shape[-1]

    def turned(ref, start, step):
        count = ref.shape[0]
        spots = lax.broadcasted_iota(jnp.int32, (count, total), 1)
        row = lax.broadcasted_iota(jnp.int32, (count, total), 0)
        place = (spots == start + (row // 8) * step + row % 8).astype(F32).astype(BF)
        return mm(split(ref[...]), (place,), TN)

    def chain(refs, right):
        out = None
        for i, ref in enumerate(refs):
            term = lax.dot_general(ref[...], right * masks[i], TN, preferred_element_type=F32)
            out = term if out is None else out + term
        return jnp.pad(out, ((0, 0), (0, total - ranks)))

    down = chain((m1_ref, m4_ref, m3_ref, m5_ref), hidden)
    up = chain((g0_ref, g1_ref, g2_ref, g3_ref), inner)
    down = down + turned(first_down_ref, ranks, 16) + turned(second_down_ref, ranks + 8, 16)
    up = up + turned(first_up_ref, ranks, 16) + turned(second_up_ref, ranks + 8, 16)
    out_ref[0] = down
    out_ref[1] = up + turned(par_ref, ranks + 16 * groups, 0)


def lowrank_grads(place, mixed, hidden, low_grads, inner, par_grad, first, second, parts):
    tokens, width = mixed[0].shape
    cols = low_grads.shape[1] // 4
    ranks = hidden.shape[1]
    block = column_block(cols)
    steps = cols // block
    groups = first.shape[0] // 8
    total = ranks + 16 * groups + 8
    side = lambda n: pl.BlockSpec((tokens, n), lambda j, at: (0, 0))
    held = [pl.BlockSpec((tokens, block), lambda j, at: (0, at[0] * steps + j))] * 4
    low = [pl.BlockSpec((tokens, block), lambda j, at, i=i: (0, i * steps + j)) for i in range(4)]
    down = pl.BlockSpec((8 * groups, block), lambda j, at: (0, j))
    up = pl.BlockSpec((8 * groups, block), lambda j, at: (0, steps + j))
    return pl.pallas_call(
        lambda *refs: lowrank_grad_kernel(parts, groups, *refs),
        name="lowrank_grads",
        grid_spec=pltpu.PrefetchScalarGridSpec(
            num_scalar_prefetch=1,
            grid=(steps,),
            in_specs=held
            + [side(ranks)]
            + low
            + [side(ranks), pl.BlockSpec((8, block), lambda j, at: (0, j)), down, up, down, up],
            out_specs=pl.BlockSpec((2, block, total), lambda j, at: (0, j, 0)),
        ),
        out_shape=jax.ShapeDtypeStruct((2, cols, total), F32),
        compiler_params=pltpu.CompilerParams(vmem_limit_bytes=48 << 20),
        cost_estimate=pl.CostEstimate(
            flops=16 * tokens * cols * ranks, bytes_accessed=5 << 20, transcendentals=0
        ),
    )(place, *mixed, hidden, *([low_grads] * 4), inner, par_grad, first, first, second, second)


def unpack_kernel(ranks, extra, given_ref, down_ref, up_ref, par_ref, totals_ref):
    rows = given_ref[:, 0].astype(F32)
    rows = rows.reshape(-1, rows.shape[-1])
    heads = rows.shape[0] // 2
    down_ref[...] = rows[:heads, :ranks]
    turned = rows.T
    up_ref[...] = turned[:ranks, heads:]
    par_ref[...] = turned[ranks + extra :, heads:]

    @pl.when(pl.program_id(0) == 0)
    def _():
        totals_ref[...] = jnp.zeros_like(totals_ref)

    totals_ref[...] += turned[ranks : ranks + extra]


def unpack(given, ranks, extra):
    size, peers, rows, total = given.shape
    heads = size * rows // 2
    width = peers * heads
    return pl.pallas_call(
        lambda *refs: unpack_kernel(ranks, extra, *refs),
        name="unpack",
        grid=(peers,),
        in_specs=[pl.BlockSpec((size, 1, rows, total), lambda p: (0, p, 0, 0))],
        out_specs=[
            pl.BlockSpec((heads, ranks), lambda p: (p, 0)),
            pl.BlockSpec((ranks, heads), lambda p: (0, p)),
            pl.BlockSpec((8, heads), lambda p: (0, p)),
            pl.BlockSpec((extra, 2 * heads), lambda p: (0, 0)),
        ],
        out_shape=[
            jax.ShapeDtypeStruct((width, ranks), F32),
            jax.ShapeDtypeStruct((ranks, width), F32),
            jax.ShapeDtypeStruct((8, width), F32),
            jax.ShapeDtypeStruct((extra, 2 * heads), F32),
        ],
        compiler_params=pltpu.CompilerParams(vmem_limit_bytes=48 << 20),
    )(given)


def halving_kernel(has_other, own_ref, *refs):
    count = len(has_other)
    given = iter(refs[: count + sum(has_other)])
    results = refs[count + sum(has_other) :]
    for i in range(count):
        held_ref = next(given)
        other_ref = next(given) if has_other[i] else None
        mine = own_ref[i]

        def half(at):
            rows = held_ref[:, at].astype(F32)
            return rows if other_ref is None else rows + other_ref[:, at].astype(F32)

        results[2 * i][...] = half(1 - mine).astype(BF)
        results[2 * i + 1][...] = half(mine).astype(BF)


def halving(own, pieces):
    steps = 4 if all(held.shape[-1] % 512 == 0 for held, _ in pieces) else 1
    operands, in_specs, out_specs, out_shape = [], [], [], []
    for held, other in pieces:
        before, _, rows, cols = held.shape
        block = cols // steps
        for x in (held, other):
            if x is not None:
                operands.append(x)
                in_specs.append(pl.BlockSpec((before, 2, rows, block), lambda j, own: (0, 0, 0, j)))
        for dtype in (BF, BF):
            out_specs.append(pl.BlockSpec((before, rows, block), lambda j, own: (0, 0, j)))
            out_shape.append(jax.ShapeDtypeStruct((before, rows, cols), dtype))
    flags = [other is not None for _, other in pieces]
    total = sum(x.size for x in operands)
    results = pl.pallas_call(
        lambda *refs: halving_kernel(flags, *refs),
        name="halving",
        grid_spec=pltpu.PrefetchScalarGridSpec(
            num_scalar_prefetch=1, grid=(steps,), in_specs=in_specs, out_specs=out_specs
        ),
        out_shape=out_shape,
        compiler_params=pltpu.CompilerParams(vmem_limit_bytes=48 << 20),
        cost_estimate=pl.CostEstimate(flops=2 * total, bytes_accessed=6 * total, transcendentals=0),
    )(own, *operands)
    return [(results[2 * i], results[2 * i + 1]) for i in range(len(pieces))]


def document_tables(segments):
    rows, length = segments.shape
    marks = segments + (length + 1) * lax.broadcasted_iota(jnp.int32, (rows, length), 0)
    flat = marks.reshape(-1).astype(F32)
    blocks = flat.reshape(-1, CHUNK)
    ends = blocks[:, -1]
    before = jnp.concatenate([jnp.full((1,), -1.0, F32), ends[:-1]])
    wide = lambda x: jnp.broadcast_to(x[:, None], (x.shape[0], PAIR))
    aux = jnp.stack([jnp.concatenate([blocks, blocks], 1), wide(ends), wide(before)] + [jnp.zeros((blocks.shape[0], PAIR), F32)] * 5, 1)
    return flat[:, None], aux


def bit_positions(size):
    return [1 << i for i in reversed(range(size.bit_length() - 1))]


def swap(x, axis, bit):
    size = lax.axis_size(axis)
    return lax.ppermute(x, axis, [(i, i ^ bit) for i in range(size)])


def power_of_two(size):
    return size & (size - 1) == 0


def gather_rows(shard, axis, order=None):
    size = lax.axis_size(axis)
    if not power_of_two(size):
        return lax.all_gather(shard, axis, axis=0, tiled=True)
    place = lax.axis_index(axis)
    bits = bit_positions(size)
    held = shard.reshape((1,) * len(bits) + shard.shape)
    for bit in order or bits:
        spot = bits.index(bit)
        other = swap(held, axis, bit)
        held = jnp.where(
            (place & bit) != 0,
            jnp.concatenate([other, held], spot),
            jnp.concatenate([held, other], spot),
        )
    return held.reshape((size * shard.shape[0],) + shard.shape[1:])


class Piece:
    def __init__(self, full, dim, axis, side_last=False):
        bits = bit_positions(lax.axis_size(axis))
        self.order = bits[::-1]
        if side_last:
            self.order = bits[-1:] + bits[:-2][::-1] + bits[-2:-1]
        self.lead, self.rows = full.shape[:dim], full.shape[dim] // lax.axis_size(axis)
        self.cols = full.shape[-1]
        self.held, self.other, self.left, self.axis = full, None, bits, axis

    def view(self, x, bit):
        spot = self.left.index(bit)
        before = 1
        for n in self.lead + (2,) * spot:
            before *= n
        return None if x is None else x.reshape(before, 2, -1, self.cols)

    def move(self, sent, bit):
        self.other = swap(sent, self.axis, bit)
        self.left = [b for b in self.left if b != bit]

    def total(self):
        shape = self.lead + (self.rows, self.cols)
        return self.held.reshape(shape) + self.other.reshape(shape).astype(F32)


def begun(pair, rows, axis, side_last=False):
    sent, kept = pair
    piece = Piece(kept, 1, axis, side_last)
    piece.rows = rows
    piece.move(sent, piece.order.pop(0))
    return piece


def prepare(*pieces):
    pieces = [piece for piece in pieces if piece.order]
    if not pieces:
        return []
    bits = [piece.order.pop(0) for piece in pieces]
    held = [(p.view(p.held, bit), p.view(p.other, bit)) for p, bit in zip(pieces, bits)]
    own = jnp.stack([((lax.axis_index(p.axis) & bit) != 0).astype(jnp.int32) for p, bit in zip(pieces, bits)])
    moves = []
    for piece, bit, (sent, kept) in zip(pieces, bits, halving(own, held)):
        piece.held = kept
        moves.append((piece, sent, bit))
    return moves


def launch(moves):
    for piece, sent, bit in moves:
        piece.move(sent, bit)


def advance(*pieces):
    launch(prepare(*pieces))


def join_peers(partial, sent, axis):
    size = lax.axis_size(axis)
    if size != 2:
        return lax.psum(partial, axis)
    return partial + swap(sent, axis, 1).astype(F32)


def add_peers(partial, axis):
    return join_peers(partial, partial.astype(BF), axis)


def scatter_peers(partial, axis):
    size = lax.axis_size(axis)
    if size != 2:
        return lax.psum_scatter(partial, axis, scatter_dimension=0, tiled=True)
    rows = partial.shape[0] // 2
    place = lax.axis_index(axis)
    sent = lax.dynamic_slice_in_dim(partial, (1 - place) * rows, rows, 0).astype(BF)
    kept = lax.dynamic_slice_in_dim(partial, place * rows, rows, 0)
    return kept + swap(sent, axis, 1).astype(F32)


def rounded(x):
    return lax.reduce_precision(x, 8, 7)


def normalized(rows):
    mean = jnp.mean(rows, -1, keepdims=True)
    centred = rows - mean
    scale = lax.rsqrt(jnp.mean(centred * centred, -1, keepdims=True) + 1e-05)
    return centred * scale, mean, scale


def norm_back(grad, unit, scale, gain):
    inner = grad * gain
    return scale * (
        inner
        - jnp.mean(inner, -1, keepdims=True)
        - unit * jnp.mean(inner * unit, -1, keepdims=True)
    )


def on_device(
    block_input,
    first_layer_values,
    segments,
    valid,
    cotangent,
    teacher,
    layer_norm_gain,
    layer_norm_bias,
    lerps,
    decay_offset,
    head_gain_table,
    per_unit_shift_array,
    lowrank_first_maps,
    lowrank_second_maps,
    receptance_key_value_weight,
    time_output_weight,
    channel_key_weight,
    channel_value_weight,
):
    tensor_size = lax.axis_size("tensor")
    tensor_pos = lax.axis_index("tensor")
    dp_pos = lax.axis_index("dp")
    own_rows, width = block_input.shape
    tokens = own_rows * tensor_size
    heads = receptance_key_value_weight.shape[2]
    units = channel_key_weight.shape[1]
    column_begin = tensor_pos * heads
    row_begin = tensor_pos * own_rows
    cut_one, cut_two = DECAY_MAP_RANK, DECAY_MAP_RANK + RATE_MAP_RANK
    cut_three = cut_two + VALUE_MIX_RANK
    ranks = lowrank_first_maps.shape[1]
    parts = ((0, DECAY_MAP_RANK), (DECAY_MAP_RANK, cut_two), (cut_two, cut_three), (cut_three, ranks))

    dp_own = (dp_pos & 1)[None].astype(jnp.int32)
    dp_rows = width // lax.axis_size("dp")
    block_low = gather_rows(block_input, "tensor")
    mixer_full = lax.all_gather(
        jnp.concatenate([w for w in receptance_key_value_weight] + [time_output_weight.T], 1),
        "dp",
        axis=0,
        tiled=True,
    )
    wide_full = lax.all_gather(
        jnp.concatenate([channel_key_weight, channel_value_weight.T], 1), "dp", axis=0, tiled=True
    )
    key_full, value_full = wide_full[:, :units], wide_full[:, units:]
    rkv_full = [mixer_full[:, i * heads : (i + 1) * heads] for i in range(3)]
    out_full = mixer_full[:, 3 * heads :]
    block_rows = block_low.astype(F32)
    teacher, cotangent, block_low = lax.optimization_barrier((teacher, cotangent, block_low))
    teacher_low = gather_rows(teacher, "tensor")
    cotangent_low = gather_rows(cotangent, "tensor")
    valid_all = valid.astype(F32).reshape(-1)
    valid_count = jnp.sum(valid_all)
    valid_rows = lax.dynamic_slice_in_dim(valid_all, dp_pos * tokens, tokens)[:, None]
    same_doc = (segments[:, 1:] == segments[:, :-1]).astype(F32)
    retain_mask = jnp.concatenate([jnp.zeros((segments.shape[0], 1), F32), same_doc], 1).reshape(-1)
    row_index = lax.broadcasted_iota(jnp.int32, (tokens, 1), 0)
    own_mask = ((row_index >= row_begin) & (row_index < row_begin + own_rows)).astype(F32)

    unit_one, mean_one, scale_one = normalized(block_rows)
    normed_one = rounded(unit_one * layer_norm_gain[0] + layer_norm_bias[0])
    delta_one = shift_down(normed_one, retain_mask) - normed_one
    blended = [(normed_one + delta_one * lerps[i]).astype(BF) for i in range(6)]
    receptance = matrix_multiply(blended[0], rkv_full[0])
    key_rows = matrix_multiply(blended[2], rkv_full[1])
    value_rows = matrix_multiply(blended[3], rkv_full[2])
    lane = lax.broadcasted_iota(jnp.int32, (1, ranks), 1)
    lanes = (1, 4, 3, 5)
    before = sum(
        matrix_multiply(
            blended[lanes[i]],
            jnp.where((lane >= parts[i][0]) & (lane < parts[i][1]), lowrank_first_maps, 0),
        )
        for i in range(4)
    )
    squashed = jnp.tanh(before)
    gated = jax.nn.sigmoid(before)
    is_decay, is_gate = lane < cut_one, lane >= cut_three
    inner = jnp.where(is_decay, squashed, jnp.where(is_gate, gated, before)).astype(BF)
    slope = jnp.where(is_decay, 1.0 - squashed * squashed, jnp.where(is_gate, gated * (1.0 - gated), 1.0))
    upper = lax.dynamic_slice_in_dim(lowrank_second_maps, column_begin, heads, 1)
    rank_row = lax.broadcasted_iota(jnp.int32, (ranks, 1), 0)
    upper_wide = jnp.concatenate(
        [jnp.where((rank_row >= a) & (rank_row < b), upper, 0) for a, b in parts], 1
    )
    low_rows = matrix_multiply(inner, upper_wide)
    par = lax.dynamic_slice_in_dim(
        jnp.concatenate([decay_offset[None], head_gain_table, per_unit_shift_array], 0),
        column_begin,
        heads,
        1,
    )
    doc_col, doc_aux = document_tables(segments)
    mixer_args = (
        receptance, key_rows, value_rows, low_rows, first_layer_values, par, doc_col, doc_aux,
    )
    mixed, *kept = mixer_forward(*mixer_args)
    mixed, teacher_low, cotangent_low = lax.optimization_barrier((mixed, teacher_low, cotangent_low))
    after_mixer = block_rows + add_peers(matrix_multiply_transposed(mixed, out_full), "tensor")
    unit_two, _, scale_two = normalized(after_mixer)
    normed_two = rounded(unit_two * layer_norm_gain[1] + layer_norm_bias[1])
    delta_two = shift_down(normed_two, retain_mask) - normed_two
    channel_in = (normed_two + delta_two * lerps[6]).astype(BF)
    rectified = jnp.maximum(matrix_multiply(channel_in, key_full), 0.0)
    hidden = (rectified * rectified).astype(BF)
    block_sum = after_mixer + add_peers(matrix_multiply_transposed(hidden, value_full), "tensor")
    block_out = lax.dynamic_slice_in_dim(block_sum, row_begin, own_rows, 0).astype(BF)
    mismatch = block_sum - teacher_low.astype(F32)
    norm = valid_count * width
    loss_part = jnp.sum(valid_rows * own_mask * mismatch * mismatch) / norm
    loss_row = jnp.full((1, width), loss_part, F32)
    seed = valid_rows * (cotangent_low.astype(F32) + 2.0 * mismatch / norm)
    seed_low = seed.astype(BF)
    pre_grad = (matrix_multiply(seed_low, value_full) * 2.0 * rectified).astype(BF)
    channel_back = matrix_multiply_transposed(pre_grad, key_full)
    lerp_six = jnp.sum(channel_back * delta_two, 0)
    spread_two = channel_back * (1.0 - lerps[6]) + shift_up(channel_back * lerps[6], retain_mask)
    gain_two = jnp.sum(spread_two * unit_two, 0)
    bias_two = jnp.sum(spread_two, 0)
    early = jnp.concatenate(
        [gain_two[None], bias_two[None], lerp_six[None], loss_row, jnp.zeros((4, width), F32)], 0
    )
    normed_two_sent = spread_two.astype(BF)
    normed_two_sent, pre_grad, seed_low = lax.optimization_barrier((normed_two_sent, pre_grad, seed_low))
    normed_two_grad = join_peers(spread_two, normed_two_sent, "tensor")
    channel_part = channel_grads(channel_in, pre_grad, seed_low, hidden)
    channel_grad = lax.psum_scatter(channel_part, "dp", scatter_dimension=1, tiled=True)
    after_grad = seed + norm_back(normed_two_grad, unit_two, scale_two, layer_norm_gain[1])
    after_low = after_grad.astype(BF)
    mixer_grad = matrix_multiply(after_low, out_full)
    recept_low, key_low, value_low, low_grads, first_grad, par_grad = mixer_backward(
        mixer_grad, *mixer_args, *kept
    )
    hidden_part = matrix_multiply_transposed(low_grads, upper_wide) * slope
    hidden_sent = hidden_part.astype(BF)
    hidden_sent, recept_low, key_low, value_low = lax.optimization_barrier(
        (hidden_sent, recept_low, key_low, value_low)
    )
    hidden_grad = join_peers(hidden_part, hidden_sent, "tensor").astype(BF)
    first_halves, second_halves = weight_grads(
        dp_own,
        dp_rows,
        (2, 2),
        [blended[0], blended[2], blended[3], after_low],
        [recept_low, key_low, value_low, mixed],
    )
    first = begun(first_halves, dp_rows, "dp")
    second = begun(second_halves, dp_rows, "dp", True)
    hidden_grad, first.other, second.other = lax.optimization_barrier(
        (hidden_grad, first.other, second.other)
    )
    advance(first, second)
    spread_one, sums = input_grads(
        block_low,
        mean_one,
        scale_one,
        retain_mask[:, None],
        layer_norm_gain[:1],
        layer_norm_bias[:1],
        lerps[:6],
        [recept_low, key_low, value_low],
        rkv_full,
        hidden_grad * own_mask.astype(BF),
        lowrank_first_maps,
        parts,
    )
    normed_one_grad = scatter_peers(spread_one, "tensor")
    groups = width // (2 * heads)

    def folded(x):
        return jnp.moveaxis(x.reshape(8, groups, 2 * heads), 1, 0).reshape(8 * groups, 2 * heads)

    low_part = lowrank_grads(
        tensor_pos[None].astype(jnp.int32),
        [blended[i] for i in lanes],
        hidden_grad,
        low_grads,
        inner,
        par_grad,
        folded(sums),
        folded(early),
        parts,
    )
    low_part, channel_grad = lax.optimization_barrier((low_part, channel_grad))
    low_piece = Piece(low_part.reshape(2 * heads, -1), 0, "dp")
    while low_piece.order:
        advance(low_piece)
        advance(first, second)
    while first.order or second.order:
        advance(first, second)
    grad_key, grad_value = channel_grad[0].astype(F32), channel_grad[1].astype(F32).T
    first_grads, second_grads = first.total(), second.total()
    grad_rkv = jnp.stack([first_grads[0], first_grads[1], second_grads[0]])
    grad_out = second_grads[1].T
    low_pair = gather_rows(low_piece.total().astype(BF)[None], "tensor")
    grad_down, grad_up, par_total, totals = unpack(gather_rows(low_pair[None], "dp"), ranks, 16 * groups)
    totals = jnp.moveaxis(totals.reshape(groups, 16, 2 * heads), 0, 1).reshape(16, width)

    def own(x):
        return lax.dynamic_slice_in_dim(x, row_begin, own_rows, 0)

    grad_in = own(after_grad) + norm_back(normed_one_grad, own(unit_one), own(scale_one), layer_norm_gain[0])
    return (
        block_out,
        totals[11, 0],
        grad_in,
        first_grad,
        jnp.stack([totals[6], totals[8]]),
        jnp.stack([totals[7], totals[9]]),
        jnp.concatenate([totals[0:1], totals[2:6], totals[10:11]], 0),
        totals[1],
        par_total[0],
        par_total[1:4],
        par_total[4:8],
        grad_down,
        grad_up,
        grad_rkv,
        grad_out,
        grad_key,
        grad_value,
    )


def solution(mesh):
    return jax.shard_map(
        on_device,
        mesh=mesh,
        in_specs=(
            P(("dp", "tensor"), None),
            P("dp", "tensor"),
            P("dp", None),
            P(),
            P(("dp", "tensor"), None),
            P(("dp", "tensor"), None),
            P(),
            P(),
            P(),
            P(),
            P(),
            P(),
            P(),
            P(),
            P(None, "dp", "tensor"),
            P("tensor", "dp"),
            P("dp", "tensor"),
            P("tensor", "dp"),
        ),
        out_specs=(
            P(("dp", "tensor"), None),
            P(),
            P(("dp", "tensor"), None),
            P("dp", "tensor"),
            P(),
            P(),
            P(),
            P(),
            P(),
            P(),
            P(),
            P(),
            P(),
            P(None, "dp", "tensor"),
            P("tensor", "dp"),
            P("dp", "tensor"),
            P("tensor", "dp"),
        ),
        check_vma=False,
    )
```
